128 devices in a mesh: slab: 32 (over z_hi, x, y), chan: 4 (over z_lo, core).
Axes of the slice: x: 4, y: 4, z: 4 (z_hi: 2, z_lo: 2; z = z_hi * 2 + z_lo), core: 2. Of those that a mesh axis runs over, the one named last changes fastest.
Arguments:
- tokens: bfloat16 [256, 32, 32, 1024], P('slab', None, None, 'chan'), may hold values from -6 to 6
- refine_feat: bfloat16 [1024, 128, 1024], P('slab', None, 'chan'), may hold values from -6 to 6
- refine_dest: int32 [1024, 1], P('slab'), may hold values from 0 to 31; in each aligned block of 32 rows (0 to 31, 32 to 63, ...) at most 2 rows name the same one
- refine_rows: int32 [1024, 128], P('slab'), may hold values from 0 to 8191
- conv_w: float32 [27, 1024], P(None, 'chan'), may hold values from -0.9 to 0.9
- norm_gain: float32 [1024], replicated, may hold values from 0.5 to 1.5
- w_val: bfloat16 [1024, 1024], P(None, 'chan'), may hold values from -0.1875 to 0.1875
- w_gate: bfloat16 [1024, 1024], P(None, 'chan'), may hold values from -0.1875 to 0.1875
- latent_keys: bfloat16 [128, 1024], replicated, may hold values from -70 to 70
- latents: float32 [128, 1024], P(None, 'chan'), may hold values from -6 to 6
Outputs:
- block_out: bfloat16 [256, 32, 32, 1024], P('slab', None, None, 'chan')
- latent_new: float32 [128, 1024], P(None, 'chan')
The draws below stay inside these ranges and needn't reach their ends.
Inputs may be any that keep to these rules, and one draw needn't show every extreme that they name: `refine_dest`: in the 32 blocks of one slab, no slab is named by more than 2 blocks. `refine_rows`: an index among the destination slab's tokens.
All inputs are finite; a program needn't handle non-finite values.
Results may differ from the reference program's by a relative error of at most 0.0035.
The reference program's roundings to bfloat16 on the way (of `mixed`, `normed`, `gated`, `assign` and `latent_state`) count: a program that leaves them out, or rounds other values in their place, can miss the bound.
Values may be sent and summed in bfloat16 or wider, within the bound.
A program may use at most 128 MiB of HBM per device.

```python
import math
import jax
import jax.numpy as jnp
import numpy as np
from jax import lax

D = 1024
LATENTS = 128
BLOCK_ROWS = 128
CZ = 8
GY = 32
GX = 32
BLK_DEV = 32
CAP = 2
ROWS_DEV = 8192
NZ = 256
N_SLAB = 32


def draw_latent_keys(key, part):
    entry_key, scale_key = jax.random.split(jax.random.fold_in(key, 17))
    entries = jnp.clip(jax.random.normal(entry_key, (LATENTS, D), jnp.float32), -4.0, 4.0)
    scales = jnp.exp(jax.random.uniform(scale_key, (LATENTS, 1), jnp.float32, math.log(0.5), math.log(2.0)))
    return (entries * scales).astype(jnp.bfloat16)


def touch_ends(result, own_key, low, high):
    longest = result.shape.index(max(result.shape))
    spots = []
    for shift in (0, 1):
        where = [jax.random.randint(jax.random.fold_in(own_key, axis), (), 0, length) for axis, length in enumerate(result.shape)]
        where[longest] = (where[longest] + shift) % result.shape[longest]
        spots.append(tuple(where))
    return result.at[spots[0]].set(low).at[spots[1]].set(high)


def level_of(key, shape, cuts, smallest, largest):
    loudness = 1.0
    for dim, shards_of in cuts:
        heights = jax.random.uniform(jax.random.fold_in(jax.random.fold_in(key, 6), dim), (shards_of,), jnp.float32, smallest / len(cuts), largest / len(cuts))
        loudness = loudness * jnp.repeat(jnp.exp(heights), shape[dim] // shards_of).reshape((-1,) + (1,) * (len(shape) - 1 - dim))
    return loudness


def assign_block(rng, own, number, rows, number_of, top, bound, slope):
    sequence = jax.random.permutation(rng, number_of)
    crowded, usual = portions_of(number_of, rows * top, bound, slope, True), portions_of(number_of, rows * top, bound, slope, False)
    places = jnp.arange(number_of)

    def named(tallies, turn):
        used = int((tallies > 0).sum())
        fixed = max(1, used // 4)
        passed = fixed + (places - fixed + turn * (used - fixed)) % max(1, number_of - fixed)
        return jnp.zeros((number_of,), jnp.int32).at[sequence[jnp.where(places < fixed, places, passed)]].set(jnp.asarray(tallies, jnp.int32))

    tallies = jnp.where(number % 4 == 0, named(crowded, number // 4), named(usual, number - number // 4 - 1))
    mixed = jax.random.permutation(jax.random.fold_in(own, 3), number_of)
    giver, sink = mixed[0:number_of // 2 * 2:2], mixed[1:number_of // 2 * 2:2]
    margin = jnp.minimum(tallies[giver] - 1, bound - tallies[sink]) // 2
    margin = jnp.where((giver == sequence[0]) | (sink == sequence[0]) | (tallies[sink] == 0), 0, jnp.maximum(margin, 0))
    passed = jax.random.randint(jax.random.fold_in(own, 4), (number_of // 2,), 0, 1 << 20) % (margin + 1)
    tallies = tallies.at[giver].add(-passed).at[sink].add(passed)
    members = jnp.searchsorted(jnp.cumsum(tallies), jnp.arange(rows * top), side="right").astype(jnp.int32)
    grid = members.reshape(top, rows).T
    grid = grid[jax.random.permutation(jax.random.fold_in(own, 1), rows)]
    turn = jax.random.randint(jax.random.fold_in(own, 2), (rows, 1), 0, top)
    return jnp.take_along_axis(grid, (jnp.arange(top)[None, :] + turn) % top, axis=1)


def portions_of(number_of, total, reach, lean, full):
    loads = [(1 << 20) // math.isqrt(grade ** lean) + 1 for grade in range(1, number_of + 1)]
    largest = reach if full else min(reach, max(-(-total // number_of), total * loads[0] // sum(loads)))
    least = 1 if total - largest >= number_of - 1 else 0
    holding, spare = [largest] + [least] * (number_of - 1), total - largest - least * (number_of - 1)
    while spare > 0:
        movable = [i for i in range(1, number_of) if holding[i] < largest] or [i for i in range(1, number_of) if holding[i] < reach]
        pool, remaining = sum([loads[i] for i in movable]), spare
        for i in movable:
            extra = min(reach - holding[i], max(1, remaining * loads[i] // pool), spare)
            holding[i] = holding[i] + extra
            spare = spare - extra
    return np.array(holding)


def noise(key, extent, width, most, cuts=(), held_as=jnp.bfloat16):
    gain = level_of(key, extent, cuts, -0.22, 0.18) if cuts else 1.0
    array = jax.random.normal(key, extent, jnp.float32) * width * gain
    return jnp.minimum(jnp.maximum(array, -most), most).astype(held_as)


def setup_inputs(seed: int = 0) -> dict:
    splits = jax.random.split(jax.random.key(seed), 11)
    tokens = noise(splits[0], (NZ, GY, GX, D), 1.0, 6.0, ((0, 32), (3, 4)))
    refine_feat = noise(splits[1], (N_SLAB * BLK_DEV, BLOCK_ROWS, D), 1.0, 6.0, ((0, 32), (2, 4)))
    refine_dest_keys = jax.random.split(jax.random.fold_in(splits[2], 1), (N_SLAB * BLK_DEV) // BLK_DEV)
    refine_dest_turns = jax.random.permutation(jax.random.fold_in(splits[2], 3), (N_SLAB * BLK_DEV) // BLK_DEV)
    refine_dest = jax.vmap(lambda own, number: assign_block(jax.random.fold_in(splits[2], 2), own, number, BLK_DEV, N_SLAB, 1, CAP, 2))(refine_dest_keys, refine_dest_turns).reshape((N_SLAB * BLK_DEV, 1))
    refine_rows = touch_ends(jax.random.randint(splits[3], (N_SLAB * BLK_DEV, BLOCK_ROWS), 0, ROWS_DEV), jax.random.fold_in(splits[3], 1), 0, ROWS_DEV - 1).astype(jnp.int32)
    conv_w = noise(splits[4], (27, D), 0.15, 0.9, ((1, 4),), jnp.float32)
    norm_gain = jnp.clip(1.0 + 0.1 * jax.random.normal(splits[5], (D,), jnp.float32), 0.5, 1.5)
    w_val = noise(splits[6], (D, D), D ** -0.5, 0.1875, ((1, 4),))
    w_gate = noise(splits[7], (D, D), D ** -0.5, 0.1875, ((1, 4),))
    latent_keys = draw_latent_keys(jax.random.fold_in(splits[10], 71), 0)
    latents = noise(splits[9], (LATENTS, D), 1.0, 6.0, ((1, 4),), jnp.float32)
    return {"tokens": tokens, "refine_feat": refine_feat, "refine_dest": refine_dest, "refine_rows": refine_rows, "conv_w": conv_w, "norm_gain": norm_gain, "w_val": w_val, "w_gate": w_gate, "latent_keys": latent_keys, "latents": latents}


def normalize(values, norm_gain):
    widened = values.astype(jnp.float32)
    meansq = lax.optimization_barrier(jnp.mean(widened * widened, axis=-1, keepdims=True))
    return (widened * lax.rsqrt(meansq + 1e-06) * norm_gain).astype(jnp.bfloat16)

def project(normed, w_val, w_gate, latent_keys):
    values = jnp.dot(normed, w_val, preferred_element_type=jnp.float32)
    gates = jnp.dot(normed, w_gate, preferred_element_type=jnp.float32)
    gated = (values * jax.nn.sigmoid(gates)).astype(jnp.bfloat16)
    scores = lax.dot_general(normed, latent_keys, (((1,), (1,)), ((), ())), preferred_element_type=jnp.float32)
    scores = scores * normed.shape[1] ** (-0.5)
    assign = jax.nn.softmax(scores, axis=-1).astype(jnp.bfloat16)
    pooled = lax.dot_general(assign, gated, (((0,), (0,)), ((), ())), preferred_element_type=jnp.float32)
    weight_total = lax.optimization_barrier(jnp.sum(assign.astype(jnp.float32), axis=0))
    return (assign, pooled, weight_total)

def reference(tokens, refine_feat, refine_dest, refine_rows, conv_w, norm_gain, w_val, w_gate, latent_keys, latents):
    targets = refine_dest[:, 0][:, None] * ROWS_DEV + refine_rows
    flat_total = NZ * GY * GX
    injected = jnp.zeros((flat_total, D), jnp.float32).at[targets.reshape(-1)].add(refine_feat.reshape(-1, D).astype(jnp.float32))
    injected = injected.reshape(N_SLAB, ROWS_DEV, D)
    framed = jnp.pad(tokens, ((1, 1), (1, 1), (1, 1), (0, 0)))
    zero_index = jnp.zeros((), jnp.int32)

    def slab_pass(inputs):
        slab_index, injected_slab = inputs
        window = lax.dynamic_slice(framed, (slab_index * CZ, zero_index, zero_index, zero_index), (CZ + 2, GY + 2, GX + 2, D))
        mixing = window[1:-1, 1:-1, 1:-1].astype(jnp.float32) + injected_slab.reshape(CZ, GY, GX, D)
        for depth in range(3):
            for across in range(3):
                for along in range(3):
                    mixing = mixing + window[depth:depth + CZ, across:across + GY, along:along + GX].astype(jnp.float32) * conv_w[depth * 9 + across * 3 + along]
        mixed = mixing.astype(jnp.bfloat16).reshape(ROWS_DEV, D)
        normed = normalize(mixed, norm_gain)
        assign, pooled, weight_total = project(normed, w_val, w_gate, latent_keys)
        return (mixed, assign, pooled, weight_total)
    slab_ids = jnp.arange(N_SLAB, dtype=jnp.int32)
    mixed_all, assign_all, pooled_all, totals_all = lax.map(slab_pass, (slab_ids, injected))
    pooled = lax.optimization_barrier(jnp.sum(pooled_all, axis=0))
    weight_total = lax.optimization_barrier(jnp.sum(totals_all, axis=0))
    latent_new = latents + pooled / (weight_total[:, None] + 1.0)
    latent_state = latent_new.astype(jnp.bfloat16)

    def read_pass(inputs):
        mixed, assign = inputs
        readback = jnp.dot(assign, latent_state, preferred_element_type=jnp.float32)
        return (mixed.astype(jnp.float32) + readback).astype(jnp.bfloat16)
    block_out = lax.map(read_pass, (mixed_all, assign_all)).reshape(NZ, GY, GX, D)
    return (block_out, latent_new)
```

```python
import functools

import jax
import jax.numpy as jnp
from jax import lax
from jax.experimental import pallas as pl
from jax.experimental.pallas import tpu as pltpu
from jax.sharding import PartitionSpec as P

MESH = pl.DeviceIdType.MESH
BF16 = jnp.bfloat16
F32 = jnp.float32
EXTRA = 8


def whole():
    return pl.BlockSpec(memory_space=pltpu.VMEM)


def pack_kernel(src_ref, feat_ref, code_ref, out_ref):
    slots, rows = out_ref.shape[0], feat_ref.shape[1]

    def one(j, carry):
        out_ref[j, pl.ds(0, rows), :] = feat_ref[src_ref[j]]
        out_ref[j, pl.ds(rows, EXTRA), :] = code_ref[j]
        return carry

    lax.fori_loop(0, slots, one, 0)


def pack(source, feat, code):
    slots = source.shape[0]
    _, rows, width = feat.shape
    return pl.pallas_call(
        pack_kernel,
        out_shape=jax.ShapeDtypeStruct((slots, rows + EXTRA, width), BF16),
        in_specs=[pl.BlockSpec(memory_space=pltpu.SMEM), whole(), whole()],
        out_specs=whole(),
        cost_estimate=pl.CostEstimate(flops=0, bytes_accessed=6 << 20, transcendentals=0),
        name="pack",
    )(source, feat, code)


def conv_kernel(tokens_ref, before_ref, after_ref, w_ref, out_ref, plane):
    z = pl.program_id(0)
    last = pl.num_programs(0) - 1
    depth, side_y, side_x, width = tokens_ref.shape

    def widen(slot, value):
        plane[slot, pl.ds(1, side_y)] = value.astype(F32)

    @pl.when(z == 0)
    def _():
        zero = jnp.zeros((side_x, width), F32)
        for slot in range(3):
            plane[slot, 0] = zero
            plane[slot, side_y + 1] = zero
        widen(2, before_ref[0])
        widen(0, tokens_ref[0])

    ahead = lax.rem(z + 1, 3)

    @pl.when(z < last)
    def _():
        widen(ahead, tokens_ref[z + 1])

    @pl.when(z == last)
    def _():
        widen(ahead, after_ref[0])

    slots = (lax.rem(z + 2, 3), lax.rem(z, 3), ahead)
    column = lax.broadcasted_iota(jnp.int32, (side_x, 128), 0)
    for half in range(width // 128):
        lanes = pl.ds(128 * half, 128)

        def one(y, carry):
            sums = [None, None, None]
            for dz in range(3):
                for dy in range(3):
                    row = plane[slots[dz], y + dy, :, lanes]
                    for dx in range(3):
                        k = 9 * dz + 3 * dy + dx
                        term = row * w_ref[pl.ds(k, 1), lanes]
                        sums[dx] = term if sums[dx] is None else sums[dx] + term
            centre = plane[slots[1], y + 1, :, lanes] + sums[1]
            left = jnp.where(column == 0, 0.0, pltpu.roll(sums[0], 1, 0))
            right = jnp.where(column == side_x - 1, 0.0, pltpu.roll(sums[2], side_x - 1, 0))
            out_ref[pl.ds(pl.multiple_of(y * side_x, side_x), side_x), lanes] = centre + left + right
            return carry

        lax.fori_loop(0, side_y, one, 0)


def conv(tokens, before, after, w):
    depth, side_y, side_x, width = tokens.shape
    rows = side_y * side_x
    fixed = lambda shape: pl.BlockSpec(shape, lambda z: (0,) * len(shape))
    return pl.pallas_call(
        conv_kernel,
        grid=(depth,),
        out_shape=jax.ShapeDtypeStruct((depth * rows, width), F32),
        in_specs=[fixed(tokens.shape), fixed(before.shape), fixed(after.shape), fixed(w.shape)],
        out_specs=pl.BlockSpec((rows, width), lambda z: (z, 0)),
        scratch_shapes=[pltpu.VMEM((3, side_y + 2, side_x, width), F32)],
        cost_estimate=pl.CostEstimate(
            flops=54 * depth * rows * width, bytes_accessed=30 << 20, transcendentals=0
        ),
        name="conv",
    )(tokens, before, after, w)


GROUP = 16


def scatter_kernel(rows_ref, clash_ref, base_ref, recv_ref, out_ref, acc, wide, feat, sems, base_sem):
    slots, block_rows = rows_ref.shape
    total, width = acc.shape
    step = 1024

    base_copy = pltpu.make_async_copy(base_ref, acc, base_sem)
    base_copy.start()

    def fetch(j):
        return pltpu.make_async_copy(
            recv_ref.at[j, pl.ds(0, block_rows)], feat.at[lax.rem(j, 4)], sems.at[lax.rem(j, 4)]
        )

    for j in range(3):
        fetch(j).start()
    base_copy.wait()

    def one(j, carry):
        fetch(j).wait()

        @pl.when(j + 3 < slots)
        def _():
            fetch(j + 3).start()

        @pl.when(rows_ref[j, 0] < total)
        def _():
            wide[...] = feat[lax.rem(j, 4)].astype(F32)

            def group(g, inner):
                first = g * GROUP
                where = [rows_ref[j, first + k] for k in range(GROUP)]
                base = pl.multiple_of(first, GROUP)

                @pl.when(clash_ref[j, g] == 0)
                def _():
                    olds = [acc[pl.ds(r, 1), :] for r in where]
                    news = [
                        old + wide[pl.ds(base + k, 1), :] for k, old in enumerate(olds)
                    ]
                    for r, new in zip(where, news):
                        acc[pl.ds(r, 1), :] = new

                @pl.when(clash_ref[j, g] != 0)
                def _():
                    for k, r in enumerate(where):
                        acc[pl.ds(r, 1), :] = acc[pl.ds(r, 1), :] + wide[pl.ds(base + k, 1), :]

                return inner

            lax.fori_loop(0, block_rows // GROUP, group, 0)

        return carry

    lax.fori_loop(0, slots, one, 0)

    def finish(i, carry):
        part = pl.ds(pl.multiple_of(i * step, step), step)
        out_ref[part, :] = acc[part, :].astype(BF16)
        return carry

    lax.fori_loop(0, total // step, finish, 0)


def scatter(rows, clash, base, recv):
    total, width = base.shape
    block_rows = rows.shape[1]
    return pl.pallas_call(
        scatter_kernel,
        out_shape=jax.ShapeDtypeStruct((total, width), BF16),
        in_specs=[
            pl.BlockSpec(memory_space=pltpu.SMEM),
            pl.BlockSpec(memory_space=pltpu.SMEM),
            pl.BlockSpec(memory_space=pl.ANY),
            pl.BlockSpec(memory_space=pl.ANY),
        ],
        out_specs=whole(),
        scratch_shapes=[
            pltpu.VMEM((total, width), F32),
            pltpu.VMEM((block_rows, width), F32),
            pltpu.VMEM((4, block_rows, width), BF16),
            pltpu.SemaphoreType.DMA((4,)),
            pltpu.SemaphoreType.DMA,
        ],
        cost_estimate=pl.CostEstimate(flops=2 << 20, bytes_accessed=16 << 20, transcendentals=0),
        name="scatter",
    )(rows, clash, base, recv)


CHUNKS = 8


def mix_kernel(
    mixed_ref,
    w_ref,
    keys_ref,
    gain_ref,
    latents_ref,
    assign_ref,
    latent_ref,
    xbuf,
    nbuf,
    wbuf,
    own,
    pooled,
    totals,
    part_out,
    part_in,
    tile_out,
    tile_in,
    new_out,
    new_in,
    local_sem,
    x_send,
    x_recv,
    w_send,
    w_recv,
    a_send,
    a_recv,
    p_send,
    p_recv,
    t_send,
    t_recv,
    n_send,
    n_recv,
):
    slab = lax.axis_index("slab")
    chan = lax.axis_index("chan")
    slabs = lax.axis_size("slab")
    z_lo, core = chan // 2, chan % 2
    peers = (
        chan,
        z_lo * 2 + (1 - core),
        (1 - z_lo) * 2 + core,
        (1 - z_lo) * 2 + (1 - core),
    )
    far_slab = (slab + slabs // 2) % slabs
    quarter = xbuf.shape[1]
    size = quarter // CHUNKS
    width = xbuf.shape[2]
    count = slabs - 1

    def local_copies():
        yield pltpu.make_async_copy(
            mixed_ref.at[pl.ds(chan * quarter, quarter)], xbuf.at[chan], local_sem.at[0]
        )
        yield pltpu.make_async_copy(w_ref, wbuf.at[chan], local_sem.at[1])

    for copy in local_copies():
        copy.start()

    barrier = pltpu.get_barrier_semaphore()
    for d in (1, 2, 3):
        pl.semaphore_signal(barrier, inc=1, device_id=(slab, peers[d]), device_id_type=MESH)
    pl.semaphore_signal(barrier, inc=1, device_id=(far_slab, peers[2]), device_id_type=MESH)

    def greet(k, carry):
        pl.semaphore_signal(
            barrier, inc=1, device_id=((slab + k) % slabs, chan), device_id_type=MESH
        )
        return carry

    lax.fori_loop(1, slabs, greet, 0)
    pl.semaphore_wait(barrier, 4 + count)

    def x_copy(d, i):
        rows = pl.ds(i * size, size)
        return pltpu.make_async_remote_copy(
            src_ref=mixed_ref.at[pl.ds(peers[d] * quarter + i * size, size)],
            dst_ref=xbuf.at[chan, rows],
            send_sem=x_send.at[d - 1, i],
            recv_sem=x_recv.at[d - 1, i],
            device_id=(slab, peers[d]),
            device_id_type=MESH,
        )

    def w_copy(which):
        source, device = (
            (w_ref, (slab, peers[1])),
            (w_ref, (far_slab, peers[2])),
            (wbuf.at[peers[2]], (slab, peers[1])),
        )[which]
        return pltpu.make_async_remote_copy(
            src_ref=source,
            dst_ref=wbuf.at[peers[2] if which == 2 else chan],
            send_sem=w_send.at[which],
            recv_sem=w_recv.at[which],
            device_id=device,
            device_id_type=MESH,
        )

    def a_copy(d, i):
        rows = pl.ds(chan * quarter + i * size, size)
        return pltpu.make_async_remote_copy(
            src_ref=own.at[pl.ds(i * size, size)],
            dst_ref=assign_ref.at[rows],
            send_sem=a_send.at[d - 1, i],
            recv_sem=a_recv.at[d - 1, i],
            device_id=(slab, peers[d]),
            device_id_type=MESH,
        )

    def start_x(i, carry):
        for d in (1, 2, 3):
            x_copy(d, i).start()
        return carry

    w_copy(1).start()
    lax.fori_loop(0, CHUNKS, start_x, 0)
    w_copy(0).start()
    pooled[...] = jnp.zeros_like(pooled)
    totals[...] = jnp.zeros_like(totals)
    for copy in local_copies():
        copy.wait()

    def assign_chunk(i):
        for d in (1, 2, 3):
            x_copy(d, i).wait_recv()
        rows = pl.ds(pl.multiple_of(i * size, size), size)
        wide = [xbuf[p, rows, :].astype(F32) for p in range(4)]
        square = sum(jnp.sum(v * v, axis=1, keepdims=True) for v in wide)
        scale = lax.rsqrt(square * (1.0 / (4 * width)) + 1e-06)
        for p in range(4):
            lanes = pl.ds(p * width, width)
            nbuf[rows, lanes] = (wide[p] * scale * gain_ref[:, lanes]).astype(BF16)
        scores = lax.dot_general(
            nbuf[rows, :], keys_ref[...], (((1,), (1,)), ((), ())), preferred_element_type=F32
        )
        scores = scores * (4 * width) ** (-0.5)
        top = jnp.max(scores, axis=1, keepdims=True)
        power = jnp.exp(scores - top)
        own[rows, :] = (power / jnp.sum(power, axis=1, keepdims=True)).astype(BF16)
        for d in (1, 2):
            a_copy(d, i).start()

    def pool_chunk(i):
        rows = pl.ds(pl.multiple_of(i * size, size), size)
        assign = own[rows, :]
        ones = jnp.ones((size, 128), BF16)
        over_rows = (((0,), (0,)), ((), ()))
        totals[...] += lax.dot_general(assign, ones, over_rows, preferred_element_type=F32)
        for p in range(4):
            both = jnp.dot(nbuf[rows, :], wbuf[p], preferred_element_type=F32)
            gated = (both[:, :width] * jax.nn.sigmoid(both[:, width:])).astype(BF16)
            pooled[p] += lax.dot_general(assign, gated, over_rows, preferred_element_type=F32)

    def early(i, carry):
        assign_chunk(i)
        return carry

    lax.fori_loop(0, CHUNKS // 2, early, 0)
    w_copy(1).wait_recv()
    w_copy(2).start()
    w_copy(0).wait_recv()
    w_copy(2).wait_recv()

    def late(i, carry):
        assign_chunk(i + CHUNKS // 2)
        pool_chunk(2 * i)
        pool_chunk(2 * i + 1)
        return carry

    lax.fori_loop(0, CHUNKS // 2, late, 0)

    keep = pltpu.make_async_copy(own, assign_ref.at[pl.ds(chan * quarter, quarter)], local_sem.at[0])
    keep.start()

    def p_copy(d):
        return pltpu.make_async_remote_copy(
            src_ref=part_out.at[peers[d]],
            dst_ref=part_in.at[d - 1],
            send_sem=p_send.at[d - 1],
            recv_sem=p_recv.at[d - 1],
            device_id=(slab, peers[d]),
            device_id_type=MESH,
        )

    for p in range(4):
        part_out[p, :, pl.ds(0, width)] = pooled[p].astype(BF16)
        part_out[p, :, pl.ds(width, 128)] = totals[...].astype(BF16)
    for d in (2, 3, 1):
        p_copy(d).start()
    for d in (1, 2, 3):
        p_copy(d).wait_recv()
    mine = pooled[chan]
    weight = totals[...]
    for d in range(3):
        mine = mine + part_in[d, :, pl.ds(0, width)].astype(F32)
        weight = weight + part_in[d, :, pl.ds(width, 128)].astype(F32)

    for t in range(slabs):
        tile = (slice(8 * (t // 2), 8 * (t // 2) + 8), slice(128 * (t % 2), 128 * (t % 2) + 128))
        tile_out[t, 0] = mine[tile]
        tile_out[t, 1] = weight[tile[0]]

    def t_copy(k):
        to = (slab + k) % slabs
        return pltpu.make_async_remote_copy(
            src_ref=tile_out.at[to],
            dst_ref=tile_in.at[slab],
            send_sem=t_send.at[k - 1],
            recv_sem=t_recv.at[k - 1],
            device_id=(to, chan),
            device_id_type=MESH,
        )

    def n_copy(k):
        return pltpu.make_async_remote_copy(
            src_ref=new_out,
            dst_ref=new_in.at[slab],
            send_sem=n_send.at[k - 1],
            recv_sem=n_recv.at[k - 1],
            device_id=((slab + k) % slabs, chan),
            device_id_type=MESH,
        )

    def over_peers(action):
        def body(k, carry):
            action(k)
            return carry

        lax.fori_loop(1, slabs, body, 0)

    over_peers(lambda k: t_copy(k).start())
    tile_in[slab] = tile_out[slab]
    over_peers(lambda k: t_copy(k).wait_recv())
    sums = jnp.sum(tile_in[...], axis=0)
    held = latents_ref[
        pl.ds(pl.multiple_of(8 * (slab // 2), 8), 8), pl.ds(pl.multiple_of(128 * (slab % 2), 128), 128)
    ]
    fresh = held + sums[0] / (sums[1] + 1.0)
    new_out[...] = fresh
    over_peers(lambda k: n_copy(k).start())
    new_in[slab] = fresh

    def forward():
        rows = pl.ds(peers[2] * quarter, quarter)
        return pltpu.make_async_remote_copy(
            src_ref=assign_ref.at[rows],
            dst_ref=assign_ref.at[rows],
            send_sem=a_send.at[2, 0],
            recv_sem=a_recv.at[2, 0],
            device_id=(slab, peers[1]),
            device_id_type=MESH,
        )

    def landed(i, carry):
        a_copy(2, i).wait_recv()
        return carry

    lax.fori_loop(0, CHUNKS, landed, 0)
    forward().start()

    over_peers(lambda k: n_copy(k).wait_recv())
    for t in range(slabs):
        latent_ref[8 * (t // 2) : 8 * (t // 2) + 8, 128 * (t % 2) : 128 * (t % 2) + 128] = new_in[t]

    def drained(i, carry):
        a_copy(1, i).wait_recv()
        for d in (1, 2):
            a_copy(d, i).wait_send()
        for d in (1, 2, 3):
            x_copy(d, i).wait_send()
        return carry

    lax.fori_loop(0, CHUNKS, drained, 0)
    for which in range(3):
        w_copy(which).wait_send()
    for d in (1, 2, 3):
        p_copy(d).wait_send()
    over_peers(lambda k: t_copy(k).wait_send())
    over_peers(lambda k: n_copy(k).wait_send())
    forward().wait()
    keep.wait()


def mix(mixed, weights, keys, gain, latents):
    rows, width = mixed.shape
    slabs = lax.axis_size("slab")
    quarter = rows // 4
    held = latents.shape[0]
    dma = pltpu.SemaphoreType.DMA
    return pl.pallas_call(
        mix_kernel,
        out_shape=(
            jax.ShapeDtypeStruct((rows, held), BF16),
            jax.ShapeDtypeStruct((held, width), F32),
        ),
        in_specs=[
            pl.BlockSpec(memory_space=pl.ANY),
            pl.BlockSpec(memory_space=pl.ANY),
            whole(),
            whole(),
            whole(),
        ],
        out_specs=(pl.BlockSpec(memory_space=pl.ANY), whole()),
        scratch_shapes=[
            pltpu.VMEM((4, quarter, width), BF16),
            pltpu.VMEM((quarter, 4 * width), BF16),
            pltpu.VMEM((4,) + weights.shape, BF16),
            pltpu.VMEM((quarter, held), BF16),
            pltpu.VMEM((4, held, width), F32),
            pltpu.VMEM((held, 128), F32),
            pltpu.VMEM((4, held, width + 128), BF16),
            pltpu.VMEM((3, held, width + 128), BF16),
            pltpu.VMEM((slabs, 2, 8, 128), F32),
            pltpu.VMEM((slabs, 2, 8, 128), F32),
            pltpu.VMEM((8, 128), F32),
            pltpu.VMEM((slabs, 8, 128), F32),
            dma((2,)),
            dma((3, CHUNKS)),
            dma((3, CHUNKS)),
            dma((3,)),
            dma((3,)),
            dma((3, CHUNKS)),
            dma((3, CHUNKS)),
            dma((3,)),
            dma((3,)),
            dma((slabs - 1,)),
            dma((slabs - 1,)),
            dma((slabs - 1,)),
            dma((slabs - 1,)),
        ],
        compiler_params=pltpu.CompilerParams(
            collective_id=0, has_side_effects=True, vmem_limit_bytes=48 << 20
        ),
        cost_estimate=pl.CostEstimate(flops=10 << 30, bytes_accessed=16 << 20, transcendentals=0),
        name="mix",
    )(mixed, weights, keys, gain, latents)


def per_device(
    tokens,
    refine_feat,
    refine_dest,
    refine_rows,
    conv_w,
    norm_gain,
    w_val,
    w_gate,
    latent_keys,
    latents,
):
    depth, side_y, side_x, width = tokens.shape
    row_count = depth * side_y * side_x
    slabs = lax.axis_size("slab")
    blocks, block_rows = refine_rows.shape
    capacity = max(2, (2 * blocks + slabs - 1) // slabs)
    slots = slabs * capacity

    targets = refine_dest[:, 0]
    ids = jnp.arange(blocks, dtype=jnp.int32)
    earlier = (targets[None, :] == targets[:, None]) & (ids[None, :] < ids[:, None])
    position = targets * capacity + jnp.sum(earlier.astype(jnp.int32), axis=1)
    chosen = position[None, :] == jnp.arange(slots, dtype=jnp.int32)[:, None]
    source = jnp.sum(jnp.where(chosen, ids[None, :], 0), axis=1)
    filled = jnp.any(chosen, axis=1)
    wanted = jnp.where(filled[:, None], refine_rows[source], row_count)
    code = jnp.concatenate([wanted // 128, wanted % 128], axis=1).astype(BF16)
    code = jnp.broadcast_to(code[:, None, :], (slots, EXTRA, width))

    up = [(i, i + 1) for i in range(slabs - 1)]
    down = [(i + 1, i) for i in range(slabs - 1)]
    before = lax.ppermute(tokens[-1:], "slab", up)
    after = lax.ppermute(tokens[:1], "slab", down)

    sent = pack(source, refine_feat, code)
    sent, before, after = lax.optimization_barrier((sent, before, after))
    received = lax.all_to_all(
        sent.reshape(slabs, capacity * (block_rows + EXTRA), width),
        "slab",
        split_axis=0,
        concat_axis=0,
        tiled=True,
    ).reshape(slots, block_rows + EXTRA, width)

    base = conv(tokens, before, after, conv_w)
    weights = jnp.concatenate([w_val, w_gate], axis=1)

    got = received[:, block_rows, :].astype(jnp.int32)
    rows = got[:, :block_rows] * 128 + got[:, block_rows:]
    grouped = rows.reshape(slots, block_rows // GROUP, GROUP)
    same = grouped[..., :, None] == grouped[..., None, :]
    above = jnp.arange(GROUP)[:, None] < jnp.arange(GROUP)[None, :]
    clash = jnp.any(same & above, axis=(2, 3)).astype(jnp.int32)

    mixed = scatter(rows, clash, base, received)
    assign, latent_new = mix(mixed, weights, latent_keys, norm_gain[None, :], latents)
    readback = jnp.dot(assign, latent_new.astype(BF16), preferred_element_type=F32)
    block_out = (mixed.astype(F32) + readback).astype(BF16)
    return (block_out.reshape(depth, side_y, side_x, width), latent_new)


def solution(mesh):
    return jax.shard_map(
        per_device,
        mesh=mesh,
        in_specs=(
            P("slab", None, None, "chan"),
            P("slab", None, "chan"),
            P("slab", None),
            P("slab", None),
            P(None, "chan"),
            P(),
            P(None, "chan"),
            P(None, "chan"),
            P(),
            P(None, "chan"),
        ),
        out_specs=(P("slab", None, None, "chan"), P(None, "chan")),
        check_vma=False,
    )
```

```python
import functools

import jax
import jax.numpy as jnp
from jax import lax
from jax.experimental import pallas as pl
from jax.experimental.pallas import tpu as pltpu
from jax.sharding import PartitionSpec as P

MESH = pl.DeviceIdType.MESH
BF16 = jnp.bfloat16
F32 = jnp.float32
EXTRA = 8


def whole():
    return pl.BlockSpec(memory_space=pltpu.VMEM)


def pack_kernel(capacity, empty, dest_ref, feat_ref, rows_ref, out_ref, taken):
    slots, width = out_ref.shape[0], out_ref.shape[2]
    blocks, rows, _ = feat_ref.shape

    def coded(number):
        both = jnp.concatenate([number // 128, number % 128], axis=1)
        return jnp.broadcast_to(both.astype(F32), (EXTRA, width)).astype(BF16)

    nothing = coded(jnp.full((1, rows), empty, jnp.int32))

    def clear(j, carry):
        out_ref[j, pl.ds(0, rows), :] = jnp.zeros((rows, width), BF16)
        out_ref[j, pl.ds(rows, EXTRA), :] = nothing
        return carry

    lax.fori_loop(0, slots, clear, 0)
    for t in range(slots // capacity):
        taken[t] = 0

    def one(b, carry):
        to = dest_ref[b]
        slot = to * capacity + taken[to]
        taken[to] = taken[to] + 1
        out_ref[slot, pl.ds(0, rows), :] = feat_ref[b]
        out_ref[slot, pl.ds(rows, EXTRA), :] = coded(rows_ref[pl.ds(b, 1), :])
        return carry

    lax.fori_loop(0, blocks, one, 0)


def pack(dest, feat, row_ids, slabs, capacity, empty):
    _, rows, width = feat.shape
    slots = slabs * capacity
    return pl.pallas_call(
        functools.partial(pack_kernel, capacity, empty),
        out_shape=jax.ShapeDtypeStruct((slots, rows + EXTRA, width), BF16),
        in_specs=[pl.BlockSpec(memory_space=pltpu.SMEM), whole(), whole()],
        out_specs=whole(),
        scratch_shapes=[pltpu.SMEM((slabs,), jnp.int32)],
        cost_estimate=pl.CostEstimate(flops=0, bytes_accessed=6 << 20, transcendentals=0),
        name="pack",
    )(dest, feat, row_ids)


def conv_kernel(tokens_ref, before_ref, after_ref, w_ref, out_ref, plane):
    z = pl.program_id(0)
    last = pl.num_programs(0) - 1
    depth, side_y, side_x, width = tokens_ref.shape

    def widen(slot, value):
        plane[slot, pl.ds(1, side_y)] = value.astype(F32)

    @pl.when(z == 0)
    def _():
        zero = jnp.zeros((side_x, width), F32)
        for slot in range(3):
            plane[slot, 0] = zero
            plane[slot, side_y + 1] = zero
        widen(2, before_ref[0])
        widen(0, tokens_ref[0])

    ahead = lax.rem(z + 1, 3)

    @pl.when(z < last)
    def _():
        widen(ahead, tokens_ref[z + 1])

    @pl.when(z == last)
    def _():
        widen(ahead, after_ref[0])

    slots = (lax.rem(z + 2, 3), lax.rem(z, 3), ahead)
    column = lax.broadcasted_iota(jnp.int32, (side_x, 128), 0)
    for half in range(width // 128):
        lanes = pl.ds(128 * half, 128)

        def one(y, carry):
            sums = [None, None, None]
            for dz in range(3):
                for dy in range(3):
                    row = plane[slots[dz], y + dy, :, lanes]
                    for dx in range(3):
                        k = 9 * dz + 3 * dy + dx
                        term = row * w_ref[pl.ds(k, 1), lanes]
                        sums[dx] = term if sums[dx] is None else sums[dx] + term
            centre = plane[slots[1], y + 1, :, lanes] + sums[1]
            left = jnp.where(column == 0, 0.0, pltpu.roll(sums[0], 1, 0))
            right = jnp.where(column == side_x - 1, 0.0, pltpu.roll(sums[2], side_x - 1, 0))
            out_ref[half, pl.ds(pl.multiple_of(y * side_x, side_x), side_x), :] = centre + left + right
            return carry

        lax.fori_loop(0, side_y, one, 0)


def conv(tokens, before, after, w):
    depth, side_y, side_x, width = tokens.shape
    rows = side_y * side_x
    fixed = lambda shape: pl.BlockSpec(shape, lambda z: (0,) * len(shape))
    return pl.pallas_call(
        conv_kernel,
        grid=(depth,),
        out_shape=jax.ShapeDtypeStruct((width // 128, depth * rows, 128), F32),
        in_specs=[fixed(tokens.shape), fixed(before.shape), fixed(after.shape), fixed(w.shape)],
        out_specs=pl.BlockSpec((width // 128, rows, 128), lambda z: (0, z, 0)),
        scratch_shapes=[pltpu.VMEM((3, side_y + 2, side_x, width), F32)],
        cost_estimate=pl.CostEstimate(
            flops=54 * depth * rows * width, bytes_accessed=30 << 20, transcendentals=0
        ),
        name="conv",
    )(tokens, before, after, w)


GROUP = 16


def scatter_kernel(
    rows_ref, clash_ref, base_ref, recv_ref, out_ref, acc0, acc1, wide, feat, feat_sems, base_sems
):
    slots, block_rows = rows_ref.shape
    total = acc0.shape[0]
    accs = (acc0, acc1)
    pieces = feat_sems.shape[0]
    each = slots // pieces
    step = 1024

    def base_copy(h):
        return pltpu.make_async_copy(base_ref.at[h], accs[h], base_sems.at[h])

    def fetch(i):
        return pltpu.make_async_copy(
            recv_ref.at[pl.ds(i * each, each), pl.ds(0, block_rows)],
            feat.at[pl.ds(i * each, each)],
            feat_sems.at[i],
        )

    for h in range(2):
        base_copy(h).start()
    for i in range(pieces):
        fetch(i).start()
    for h in range(2):
        base_copy(h).wait()

    def add_row(j, c, offset):
        r = rows_ref[j, c]
        for h in range(2):
            accs[h][pl.ds(r, 1), :] = (
                accs[h][pl.ds(r, 1), :] + wide[h, pl.ds(offset, 1), :]
            )

    def one(j, carry):
        @pl.when(lax.rem(j, each) == 0)
        def _():
            fetch(j // each).wait()

        @pl.when(rows_ref[j, 0] < total)
        def _():
            for h in range(2):
                wide[h] = feat[j, :, pl.ds(128 * h, 128)].astype(F32)

            for g in range(block_rows // GROUP):
                first = g * GROUP

                @pl.when(clash_ref[j, g] == 0)
                def _():
                    where = [rows_ref[j, first + k] for k in range(GROUP)]
                    news = [
                        [
                            accs[h][pl.ds(r, 1), :]
                            + wide[h, first + k : first + k + 1, :]
                            for h in range(2)
                        ]
                        for k, r in enumerate(where)
                    ]
                    for r, new in zip(where, news):
                        for h in range(2):
                            accs[h][pl.ds(r, 1), :] = new[h]

                @pl.when(clash_ref[j, g] != 0)
                def _():
                    def single(k, inner):
                        add_row(j, first + k, first + k)
                        return inner

                    lax.fori_loop(0, GROUP, single, 0)

        return carry

    lax.fori_loop(0, slots, one, 0)

    def finish(i, carry):
        part = pl.ds(pl.multiple_of(i * step, step), step)
        for h in range(2):
            out_ref[part, pl.ds(128 * h, 128)] = accs[h][part, :].astype(BF16)
        return carry

    lax.fori_loop(0, total // step, finish, 0)


def scatter(rows, clash, base, recv):
    _, total, lanes = base.shape
    slots, block_rows = rows.shape
    width = 2 * lanes
    return pl.pallas_call(
        scatter_kernel,
        out_shape=jax.ShapeDtypeStruct((total, width), BF16),
        in_specs=[
            pl.BlockSpec(memory_space=pltpu.SMEM),
            pl.BlockSpec(memory_space=pltpu.SMEM),
            pl.BlockSpec(memory_space=pl.ANY),
            pl.BlockSpec(memory_space=pl.ANY),
        ],
        out_specs=whole(),
        scratch_shapes=[
            pltpu.VMEM((total, lanes), F32),
            pltpu.VMEM((total, lanes), F32),
            pltpu.VMEM((2, block_rows, lanes), F32),
            pltpu.VMEM((slots, block_rows, width), BF16),
            pltpu.SemaphoreType.DMA((8,)),
            pltpu.SemaphoreType.DMA((2,)),
        ],
        cost_estimate=pl.CostEstimate(flops=2 << 20, bytes_accessed=16 << 20, transcendentals=0),
        name="scatter",
    )(rows, clash, base, recv)


CHUNKS = 8


def mix_kernel(
    mixed_ref,
    w_ref,
    keys_ref,
    gain_ref,
    latents_ref,
    assign_ref,
    latent_ref,
    xbuf,
    nbuf,
    wbuf,
    own,
    pooled,
    totals,
    part_out,
    part_in,
    tile_out,
    tile_in,
    new_out,
    new_in,
    local_sem,
    x_send,
    x_recv,
    w_send,
    w_recv,
    a_send,
    a_recv,
    p_send,
    p_recv,
    t_send,
    t_recv,
    n_send,
    n_recv,
):
    slab = lax.axis_index("slab")
    chan = lax.axis_index("chan")
    slabs = lax.axis_size("slab")
    z_lo, core = chan // 2, chan % 2
    peers = (
        chan,
        z_lo * 2 + (1 - core),
        (1 - z_lo) * 2 + core,
        (1 - z_lo) * 2 + (1 - core),
    )
    far_slab = (slab + slabs // 2) % slabs
    quarter = xbuf.shape[1]
    size = quarter // CHUNKS
    width = xbuf.shape[2]
    half = slabs // 2
    z_hi, spot = slab // half, slab % half

    def local_copies():
        yield pltpu.make_async_copy(
            mixed_ref.at[pl.ds(chan * quarter, quarter)], xbuf.at[chan], local_sem.at[0]
        )
        yield pltpu.make_async_copy(w_ref, wbuf.at[chan], local_sem.at[1])

    for copy in local_copies():
        copy.start()

    barrier = pltpu.get_barrier_semaphore()
    for d in (1, 2, 3):
        for where in (slab, far_slab):
            pl.semaphore_signal(barrier, inc=1, device_id=(where, peers[d]), device_id_type=MESH)

    def greet(k, carry):
        pl.semaphore_signal(
            barrier, inc=1, device_id=((slab + k) % slabs, chan), device_id_type=MESH
        )
        return carry

    lax.fori_loop(1, slabs, greet, 0)
    pl.semaphore_wait(barrier, 6 + slabs - 1)

    def x_copy(d, i):
        rows = pl.ds(i * size, size)
        return pltpu.make_async_remote_copy(
            src_ref=mixed_ref.at[pl.ds(peers[d] * quarter + i * size, size)],
            dst_ref=xbuf.at[chan, rows],
            send_sem=x_send.at[d - 1, i],
            recv_sem=x_recv.at[d - 1, i],
            device_id=(slab, peers[d]),
            device_id_type=MESH,
        )

    def w_copy(which):
        source, device = (
            (w_ref, (slab, peers[1])),
            (w_ref, (far_slab, peers[2])),
            (wbuf.at[peers[2]], (slab, peers[1])),
        )[which]
        return pltpu.make_async_remote_copy(
            src_ref=source,
            dst_ref=wbuf.at[peers[2] if which == 2 else chan],
            send_sem=w_send.at[which],
            recv_sem=w_recv.at[which],
            device_id=device,
            device_id_type=MESH,
        )

    def a_copy(d):
        return pltpu.make_async_remote_copy(
            src_ref=own,
            dst_ref=assign_ref.at[pl.ds(chan * quarter, quarter)],
            send_sem=a_send.at[d - 1],
            recv_sem=a_recv.at[d - 1],
            device_id=(slab, peers[d]),
            device_id_type=MESH,
        )

    def start_x(i, carry):
        for d in (1, 2, 3):
            x_copy(d, i).start()
        return carry

    w_copy(1).start()
    lax.fori_loop(0, CHUNKS, start_x, 0)
    w_copy(0).start()
    pooled[...] = jnp.zeros_like(pooled)
    totals[...] = jnp.zeros_like(totals)
    for copy in local_copies():
        copy.wait()

    def assign_chunk(i):
        for d in (1, 2, 3):
            x_copy(d, i).wait_recv()
        rows = pl.ds(pl.multiple_of(i * size, size), size)
        wide = [xbuf[p, rows, :].astype(F32) for p in range(4)]
        square = sum(jnp.sum(v * v, axis=1, keepdims=True) for v in wide)
        scale = lax.rsqrt(square * (1.0 / (4 * width)) + 1e-06)
        for p in range(4):
            lanes = pl.ds(p * width, width)
            nbuf[rows, lanes] = (wide[p] * scale * gain_ref[:, lanes]).astype(BF16)
        scores = lax.dot_general(
            nbuf[rows, :], keys_ref[...], (((1,), (1,)), ((), ())), preferred_element_type=F32
        )
        scores = scores * (4 * width) ** (-0.5)
        top = jnp.max(scores, axis=1, keepdims=True)
        power = jnp.exp(scores - top)
        own[rows, :] = (power / jnp.sum(power, axis=1, keepdims=True)).astype(BF16)

    def pool_chunk(i):
        rows = pl.ds(pl.multiple_of(i * size, size), size)
        assign = own[rows, :]
        over_rows = (((0,), (0,)), ((), ()))
        totals[...] += jnp.dot(jnp.ones((16, size), BF16), assign, preferred_element_type=F32)
        for p in range(4):
            both = jnp.dot(nbuf[rows, :], wbuf[p], preferred_element_type=F32)
            gated = (both[:, :width] * jax.nn.sigmoid(both[:, width:])).astype(BF16)
            pooled[p] += lax.dot_general(assign, gated, over_rows, preferred_element_type=F32)

    def early(i, carry):
        assign_chunk(i)
        return carry

    lax.fori_loop(0, CHUNKS // 2, early, 0)
    w_copy(1).wait_recv()
    w_copy(2).start()
    w_copy(0).wait_recv()
    w_copy(2).wait_recv()

    def late(i, carry):
        assign_chunk(i + CHUNKS // 2)
        pool_chunk(2 * i)
        pool_chunk(2 * i + 1)
        return carry

    lax.fori_loop(0, CHUNKS // 2 - 1, late, 0)
    pool_chunk(CHUNKS - 2)
    assign_chunk(CHUNKS - 1)
    pool_chunk(CHUNKS - 1)

    column = [(far, d) for far in range(2) for d in range(4)][1:]
    held = pooled.shape[1] // 2

    def p_copy(n):
        far, d = column[n]
        return pltpu.make_async_remote_copy(
            src_ref=part_out.at[(z_hi + far) % 2, peers[d]],
            dst_ref=part_in.at[n],
            send_sem=p_send.at[n],
            recv_sem=p_recv.at[n],
            device_id=((slab + far * half) % slabs, peers[d]),
            device_id_type=MESH,
        )

    weights = totals[...]
    for p in range(4):
        for h in range(2):
            part_out[h, p, pl.ds(0, held)] = pooled[p, pl.ds(h * held, held)].astype(BF16)
            part_out[h, p, pl.ds(held, 16), pl.ds(0, 128)] = weights.astype(BF16)
            part_out[h, p, pl.ds(held, 16), pl.ds(128, width - 128)] = jnp.zeros(
                (16, width - 128), BF16
            )
    for n in (1, 2, 3, 4, 5, 6, 0):
        p_copy(n).start()
    for d in (2, 1):
        a_copy(d).start()
    keep = pltpu.make_async_copy(own, assign_ref.at[pl.ds(chan * quarter, quarter)], local_sem.at[0])
    keep.start()
    for n in range(7):
        p_copy(n).wait_recv()
    mine = pooled[chan, pl.ds(pl.multiple_of(z_hi * held, held), held)]
    for n in range(7):
        mine = mine + part_in[n, pl.ds(0, held)].astype(F32)
        weights = weights + part_in[n, pl.ds(held, 16), pl.ds(0, 128)].astype(F32)

    for t in range(half):
        tile_out[t, 0] = mine[8 * (t // 2) : 8 * (t // 2) + 8, 128 * (t % 2) : 128 * (t % 2) + 128]
        tile_out[t, 1] = weights[:8]

    def t_copy(k):
        to = (spot + k) % half
        return pltpu.make_async_remote_copy(
            src_ref=tile_out.at[to],
            dst_ref=tile_in.at[spot],
            send_sem=t_send.at[k - 1],
            recv_sem=t_recv.at[k - 1],
            device_id=(z_hi * half + to, chan),
            device_id_type=MESH,
        )

    def n_copy(k):
        return pltpu.make_async_remote_copy(
            src_ref=new_out,
            dst_ref=new_in.at[slab],
            send_sem=n_send.at[k - 1],
            recv_sem=n_recv.at[k - 1],
            device_id=((slab + k) % slabs, chan),
            device_id_type=MESH,
        )

    def over(number, action):
        def body(k, carry):
            action(k)
            return carry

        lax.fori_loop(1, number, body, 0)

    over(half, lambda k: t_copy(k).start())
    tile_in[spot] = tile_out[spot]
    over(half, lambda k: t_copy(k).wait_recv())
    sums = jnp.sum(tile_in[...], axis=0)
    first = z_hi * held + 8 * (spot // 2)
    row = lax.broadcasted_iota(jnp.int32, (8, 128), 0)
    lane = lax.broadcasted_iota(jnp.int32, (8, 128), 1)
    weight = jnp.sum(jnp.where(lane == row + first, sums[1], 0.0), axis=1, keepdims=True)
    before = latents_ref[
        pl.ds(pl.multiple_of(first, 8), 8), pl.ds(pl.multiple_of(128 * (spot % 2), 128), 128)
    ]
    fresh = before + sums[0] / (weight + 1.0)
    new_out[...] = fresh
    over(slabs, lambda k: n_copy(k).start())
    new_in[slab] = fresh

    def forward():
        rows = pl.ds(peers[2] * quarter, quarter)
        return pltpu.make_async_remote_copy(
            src_ref=assign_ref.at[rows],
            dst_ref=assign_ref.at[rows],
            send_sem=a_send.at[2],
            recv_sem=a_recv.at[2],
            device_id=(slab, peers[1]),
            device_id_type=MESH,
        )

    a_copy(2).wait_recv()
    forward().start()

    over(slabs, lambda k: n_copy(k).wait_recv())
    for t in range(slabs):
        top, left = held * (t // half) + 8 * ((t % half) // 2), 128 * (t % 2)
        latent_ref[top : top + 8, left : left + 128] = new_in[t]

    def drained(i, carry):
        for d in (1, 2, 3):
            x_copy(d, i).wait_send()
        return carry

    lax.fori_loop(0, CHUNKS, drained, 0)
    for which in range(3):
        w_copy(which).wait_send()
    for n in range(7):
        p_copy(n).wait_send()
    over(half, lambda k: t_copy(k).wait_send())
    over(slabs, lambda k: n_copy(k).wait_send())
    a_copy(1).wait_recv()
    for d in (1, 2):
        a_copy(d).wait_send()
    forward().wait()
    keep.wait()


def mix(mixed, weights, keys, gain, latents):
    rows, width = mixed.shape
    slabs = lax.axis_size("slab")
    quarter = rows // 4
    held = latents.shape[0]
    dma = pltpu.SemaphoreType.DMA
    return pl.pallas_call(
        mix_kernel,
        out_shape=(
            jax.ShapeDtypeStruct((rows, held), BF16),
            jax.ShapeDtypeStruct((held, width), F32),
        ),
        in_specs=[
            pl.BlockSpec(memory_space=pl.ANY),
            pl.BlockSpec(memory_space=pl.ANY),
            whole(),
            whole(),
            whole(),
        ],
        out_specs=(pl.BlockSpec(memory_space=pl.ANY), whole()),
        scratch_shapes=[
            pltpu.VMEM((4, quarter, width), BF16),
            pltpu.VMEM((quarter, 4 * width), BF16),
            pltpu.VMEM((4,) + weights.shape, BF16),
            pltpu.VMEM((quarter, held), BF16),
            pltpu.VMEM((4, held, width), F32),
            pltpu.VMEM((16, 128), F32),
            pltpu.VMEM((2, 4, held // 2 + 16, width), BF16),
            pltpu.VMEM((7, held // 2 + 16, width), BF16),
            pltpu.VMEM((slabs // 2, 2, 8, 128), F32),
            pltpu.VMEM((slabs // 2, 2, 8, 128), F32),
            pltpu.VMEM((8, 128), F32),
            pltpu.VMEM((slabs, 8, 128), F32),
            dma((2,)),
            dma((3, CHUNKS)),
            dma((3, CHUNKS)),
            dma((3,)),
            dma((3,)),
            dma((3,)),
            dma((3,)),
            dma((7,)),
            dma((7,)),
            dma((slabs // 2 - 1,)),
            dma((slabs // 2 - 1,)),
            dma((slabs - 1,)),
            dma((slabs - 1,)),
        ],
        compiler_params=pltpu.CompilerParams(
            collective_id=0, has_side_effects=True, vmem_limit_bytes=48 << 20
        ),
        cost_estimate=pl.CostEstimate(flops=10 << 30, bytes_accessed=16 << 20, transcendentals=0),
        name="mix",
    )(mixed, weights, keys, gain, latents)


def per_device(
    tokens,
    refine_feat,
    refine_dest,
    refine_rows,
    conv_w,
    norm_gain,
    w_val,
    w_gate,
    latent_keys,
    latents,
):
    depth, side_y, side_x, width = tokens.shape
    row_count = depth * side_y * side_x
    slabs = lax.axis_size("slab")
    blocks, block_rows = refine_rows.shape
    capacity = max(2, (2 * blocks + slabs - 1) // slabs)
    slots = slabs * capacity

    up = [(i, i + 1) for i in range(slabs - 1)]
    down = [(i + 1, i) for i in range(slabs - 1)]
    before = lax.ppermute(tokens[-1:], "slab", up)
    after = lax.ppermute(tokens[:1], "slab", down)

    sent = pack(refine_dest[:, 0], refine_feat, refine_rows, slabs, capacity, row_count)
    sent, before, after = lax.optimization_barrier((sent, before, after))
    received = lax.all_to_all(
        sent.reshape(slabs, capacity * (block_rows + EXTRA), width),
        "slab",
        split_axis=0,
        concat_axis=0,
        tiled=True,
    ).reshape(slots, block_rows + EXTRA, width)

    base = conv(tokens, before, after, conv_w)
    weights = jnp.concatenate([w_val, w_gate], axis=1)

    got = received[:, block_rows, :].astype(jnp.int32)
    rows = got[:, :block_rows] * 128 + got[:, block_rows:]
    grouped = rows.reshape(slots, block_rows // GROUP, GROUP)
    same = grouped[..., :, None] == grouped[..., None, :]
    above = jnp.arange(GROUP)[:, None] < jnp.arange(GROUP)[None, :]
    clash = jnp.any(same & above, axis=(2, 3)).astype(jnp.int32)

    mixed = scatter(rows, clash, base, received)
    assign, latent_new = mix(mixed, weights, latent_keys, norm_gain[None, :], latents)
    readback = jnp.dot(assign, latent_new.astype(BF16), preferred_element_type=F32)
    block_out = (mixed.astype(F32) + readback).astype(BF16)
    return (block_out.reshape(depth, side_y, side_x, width), latent_new)


def solution(mesh):
    return jax.shard_map(
        per_device,
        mesh=mesh,
        in_specs=(
            P("slab", None, None, "chan"),
            P("slab", None, "chan"),
            P("slab", None),
            P("slab", None),
            P(None, "chan"),
            P(),
            P(None, "chan"),
            P(None, "chan"),
            P(),
            P(None, "chan"),
        ),
        out_specs=(P("slab", None, None, "chan"), P(None, "chan")),
        check_vma=False,
    )
```

```python
import functools

import jax
import jax.numpy as jnp
from jax import lax
from jax.experimental import pallas as pl
from jax.experimental.pallas import tpu as pltpu
from jax.sharding import PartitionSpec as P


MESH = pl.DeviceIdType.MESH
BF16 = jnp.bfloat16
F32 = jnp.float32
EXTRA = 8


def whole():
    return pl.BlockSpec(memory_space=pltpu.VMEM)


def pack_kernel(capacity, empty, dest_ref, feat_ref, rows_ref, out_ref, taken):
    slots, width = out_ref.shape[0], out_ref.shape[2]
    blocks, rows, _ = feat_ref.shape

    def coded(number):
        both = jnp.concatenate([number // 128, number % 128], axis=1)
        return jnp.broadcast_to(both.astype(F32), (EXTRA, width)).astype(BF16)

    nothing = coded(jnp.full((1, rows), empty, jnp.int32))

    def clear(j, carry):
        out_ref[j, pl.ds(0, rows), :] = jnp.zeros((rows, width), BF16)
        out_ref[j, pl.ds(rows, EXTRA), :] = nothing
        return carry

    lax.fori_loop(0, slots, clear, 0)
    for t in range(slots // capacity):
        taken[t] = 0

    def one(b, carry):
        to = dest_ref[b]
        slot = to * capacity + taken[to]
        taken[to] = taken[to] + 1
        out_ref[slot, pl.ds(0, rows), :] = feat_ref[b]
        out_ref[slot, pl.ds(rows, EXTRA), :] = coded(rows_ref[pl.ds(b, 1), :])
        return carry

    lax.fori_loop(0, blocks, one, 0)


def pack(dest, feat, row_ids, slabs, capacity, empty):
    _, rows, width = feat.shape
    slots = slabs * capacity
    return pl.pallas_call(
        functools.partial(pack_kernel, capacity, empty),
        out_shape=jax.ShapeDtypeStruct((slots, rows + EXTRA, width), BF16),
        in_specs=[pl.BlockSpec(memory_space=pltpu.SMEM), whole(), whole()],
        out_specs=whole(),
        scratch_shapes=[pltpu.SMEM((slabs,), jnp.int32)],
        cost_estimate=pl.CostEstimate(flops=0, bytes_accessed=6 << 20, transcendentals=0),
        name="pack",
    )(dest, feat, row_ids)


def conv_kernel(tokens_ref, before_ref, after_ref, w_ref, out_ref, plane):
    z = pl.program_id(0)
    last = pl.num_programs(0) - 1
    _, side_y, side_x, width = tokens_ref.shape

    def widen(slot, value):
        plane[slot, pl.ds(1, side_y)] = value.astype(F32)

    @pl.when(z == 0)
    def _():
        zero = jnp.zeros((side_x, width), F32)
        for slot in range(3):
            plane[slot, 0] = zero
            plane[slot, side_y + 1] = zero
        widen(2, before_ref[0])
        widen(0, tokens_ref[0])

    ahead = lax.rem(z + 1, 3)

    @pl.when(z < last)
    def _():
        widen(ahead, tokens_ref[z + 1])

    @pl.when(z == last)
    def _():
        widen(ahead, after_ref[0])

    slots = (lax.rem(z + 2, 3), lax.rem(z, 3), ahead)
    column = lax.broadcasted_iota(jnp.int32, (side_x, 128), 0)
    for half in range(width // 128):
        lanes = pl.ds(128 * half, 128)

        def one(y, carry):
            sums = [None, None, None]
            for dz in range(3):
                for dy in range(3):
                    row = plane[slots[dz], y + dy, :, lanes]
                    for dx in range(3):
                        k = 9 * dz + 3 * dy + dx
                        term = row * w_ref[pl.ds(k, 1), lanes]
                        sums[dx] = term if sums[dx] is None else sums[dx] + term
            centre = plane[slots[1], y + 1, :, lanes] + sums[1]
            left = jnp.where(column == 0, 0.0, pltpu.roll(sums[0], 1, 0))
            right = jnp.where(column == side_x - 1, 0.0, pltpu.roll(sums[2], side_x - 1, 0))
            value = centre + left + right
            for i in range(0, side_x, 8):
                to = pl.ds(pl.multiple_of(2 * side_x * y + 2 * i + 8 * half, 8), 8)
                out_ref[to, :] = value[i : i + 8]
            return carry

        lax.fori_loop(0, side_y, one, 0)


def conv(tokens, before, after, w):
    depth, side_y, side_x, width = tokens.shape
    rows = side_y * side_x
    fixed = lambda shape: pl.BlockSpec(shape, lambda z: (0,) * len(shape))
    return pl.pallas_call(
        conv_kernel,
        grid=(depth,),
        out_shape=jax.ShapeDtypeStruct((2 * depth * rows, 128), F32),
        in_specs=[fixed(tokens.shape), fixed(before.shape), fixed(after.shape), fixed(w.shape)],
        out_specs=pl.BlockSpec((2 * rows, 128), lambda z: (z, 0)),
        scratch_shapes=[pltpu.VMEM((3, side_y + 2, side_x, width), F32)],
        cost_estimate=pl.CostEstimate(
            flops=54 * depth * rows * width, bytes_accessed=30 << 20, transcendentals=0
        ),
        name="conv",
    )(tokens, before, after, w)


GROUP = 16


def scatter_kernel(
    spots_ref, clash_ref, base_ref, recv_ref, out_ref, acc, wide, feat, feat_sems, base_sem
):
    slots, block_rows = spots_ref.shape
    total = acc.shape[0] // 2
    pieces = feat_sems.shape[0]
    each = slots // pieces
    step = 128

    base_copy = pltpu.make_async_copy(base_ref, acc, base_sem)

    def fetch(i):
        return pltpu.make_async_copy(
            recv_ref.at[pl.ds(i * each, each), pl.ds(0, block_rows)],
            feat.at[pl.ds(i * each, each)],
            feat_sems.at[i],
        )

    base_copy.start()
    for i in range(pieces):
        fetch(i).start()
    base_copy.wait()

    def at(spot):
        return pl.ds(spot, 2, stride=8)

    def one(j, carry):
        @pl.when(lax.rem(j, each) == 0)
        def _():
            fetch(j // each).wait()

        @pl.when(spots_ref[j, 0] < 2 * total)
        def _():
            for k in range(0, block_rows, 16):
                for h in range(2):
                    value = feat[j, k : k + 16, 128 * h : 128 * h + 128].astype(F32)
                    wide[2 * k + 8 * h : 2 * k + 8 * h + 8, :] = value[:8]
                    wide[2 * k + 16 + 8 * h : 2 * k + 24 + 8 * h, :] = value[8:]

            groups = block_rows // GROUP
            mine = [2 * (c - c % 8) + c % 8 for c in range(block_rows)]

            def together(g):
                places = range(g * GROUP, (g + 1) * GROUP)
                where = [spots_ref[j, c] for c in places]
                news = [acc[at(r), :] + wide[at(mine[c]), :] for r, c in zip(where, places)]
                for r, new in zip(where, news):
                    acc[at(r), :] = new

            @pl.when(clash_ref[j, groups] == 0)
            def _():
                for g in range(groups):
                    together(g)

            @pl.when(clash_ref[j, groups] != 0)
            def _():
                for g in range(groups):

                    @pl.when(clash_ref[j, g] == 0)
                    def _():
                        together(g)

                    @pl.when(clash_ref[j, g] != 0)
                    def _():
                        for c in range(g * GROUP, (g + 1) * GROUP):
                            r = spots_ref[j, c]
                            acc[at(r), :] = acc[at(r), :] + wide[at(mine[c]), :]

        return carry

    lax.fori_loop(0, slots, one, 0)

    def finish(i, carry):
        value = acc[pl.ds(pl.multiple_of(i * 2 * step, 2 * step), 2 * step), :]
        value = value.reshape(step // 8, 2, 8, 128)
        part = pl.ds(pl.multiple_of(i * step, step), step)
        for h in range(2):
            out_ref[part, 128 * h : 128 * h + 128] = value[:, h].reshape(step, 128).astype(BF16)
        return carry

    lax.fori_loop(0, total // step, finish, 0)


def scatter(spots, clash, base, recv):
    total, width = base.shape[0] // 2, 2 * base.shape[1]
    slots, block_rows = spots.shape
    return pl.pallas_call(
        scatter_kernel,
        out_shape=jax.ShapeDtypeStruct((total, width), BF16),
        in_specs=[
            pl.BlockSpec(memory_space=pltpu.SMEM),
            pl.BlockSpec(memory_space=pltpu.SMEM),
            pl.BlockSpec(memory_space=pl.ANY),
            pl.BlockSpec(memory_space=pl.ANY),
        ],
        out_specs=whole(),
        scratch_shapes=[
            pltpu.VMEM((2 * total, 128), F32),
            pltpu.VMEM((2 * block_rows, 128), F32),
            pltpu.VMEM((slots, block_rows, width), BF16),
            pltpu.SemaphoreType.DMA((8,)),
            pltpu.SemaphoreType.DMA,
        ],
        cost_estimate=pl.CostEstimate(flops=2 << 20, bytes_accessed=16 << 20, transcendentals=0),
        name="scatter",
    )(spots, clash, base, recv)


CHUNKS = 8


def mix_kernel(
    mixed_ref,
    w_ref,
    keys_ref,
    gain_ref,
    latents_ref,
    assign_ref,
    latent_ref,
    xbuf,
    nbuf,
    wbuf,
    own,
    pooled,
    totals,
    part_out,
    part_in,
    tile_out,
    tile_in,
    new_out,
    new_in,
    local_sem,
    x_send,
    x_recv,
    w_send,
    w_recv,
    a_send,
    a_recv,
    p_send,
    p_recv,
    t_send,
    t_recv,
    n_send,
    n_recv,
):
    slab = lax.axis_index("slab")
    chan = lax.axis_index("chan")
    slabs = lax.axis_size("slab")
    z_lo, core = chan // 2, chan % 2
    peers = (
        chan,
        z_lo * 2 + (1 - core),
        (1 - z_lo) * 2 + core,
        (1 - z_lo) * 2 + (1 - core),
    )
    far_slab = (slab + slabs // 2) % slabs
    quarter = xbuf.shape[1]
    size = quarter // CHUNKS
    width = xbuf.shape[2]
    half = slabs // 2
    z_hi, spot = slab // half, slab % half

    def local_copies():
        yield pltpu.make_async_copy(
            mixed_ref.at[pl.ds(chan * quarter, quarter)], xbuf.at[chan], local_sem.at[0]
        )
        yield pltpu.make_async_copy(w_ref, wbuf.at[chan], local_sem.at[1])

    for copy in local_copies():
        copy.start()

    barrier = pltpu.get_barrier_semaphore()
    for d in (1, 2, 3):
        for where in (slab, far_slab):
            pl.semaphore_signal(barrier, inc=1, device_id=(where, peers[d]), device_id_type=MESH)

    def greet(k, carry):
        pl.semaphore_signal(
            barrier, inc=1, device_id=((slab + k) % slabs, chan), device_id_type=MESH
        )
        return carry

    lax.fori_loop(1, slabs, greet, 0)
    pl.semaphore_wait(barrier, 6 + slabs - 1)

    def x_copy(d, i):
        rows = pl.ds(i * size, size)
        return pltpu.make_async_remote_copy(
            src_ref=mixed_ref.at[pl.ds(peers[d] * quarter + i * size, size)],
            dst_ref=xbuf.at[chan, rows],
            send_sem=x_send.at[d - 1, i],
            recv_sem=x_recv.at[d - 1, i],
            device_id=(slab, peers[d]),
            device_id_type=MESH,
        )

    def w_copy(which):
        source, device = (
            (w_ref, (slab, peers[1])),
            (w_ref, (far_slab, peers[2])),
            (wbuf.at[peers[2]], (slab, peers[1])),
        )[which]
        return pltpu.make_async_remote_copy(
            src_ref=source,
            dst_ref=wbuf.at[peers[2] if which == 2 else chan],
            send_sem=w_send.at[which],
            recv_sem=w_recv.at[which],
            device_id=device,
            device_id_type=MESH,
        )

    def a_copy(d):
        return pltpu.make_async_remote_copy(
            src_ref=own,
            dst_ref=assign_ref.at[pl.ds(chan * quarter, quarter)],
            send_sem=a_send.at[d - 1],
            recv_sem=a_recv.at[d - 1],
            device_id=(slab, peers[d]),
            device_id_type=MESH,
        )

    def start_x(i, carry):
        for d in (1, 2, 3):
            x_copy(d, i).start()
        return carry

    w_copy(1).start()
    lax.fori_loop(0, CHUNKS, start_x, 0)
    w_copy(0).start()
    pooled[...] = jnp.zeros_like(pooled)
    totals[...] = jnp.zeros_like(totals)
    for copy in local_copies():
        copy.wait()

    def assign_chunk(i):
        for d in (1, 2, 3):
            x_copy(d, i).wait_recv()
        rows = pl.ds(pl.multiple_of(i * size, size), size)
        wide = [xbuf[p, rows, :].astype(F32) for p in range(4)]
        square = sum(jnp.sum(v * v, axis=1, keepdims=True) for v in wide)
        scale = lax.rsqrt(square * (1.0 / (4 * width)) + 1e-06)
        for p in range(4):
            lanes = pl.ds(p * width, width)
            nbuf[rows, lanes] = (wide[p] * scale * gain_ref[:, lanes]).astype(BF16)
        scores = lax.dot_general(
            nbuf[rows, :], keys_ref[...], (((1,), (1,)), ((), ())), preferred_element_type=F32
        )
        scores = scores * (4 * width) ** (-0.5)
        top = jnp.max(scores, axis=1, keepdims=True)
        power = jnp.exp(scores - top)
        own[rows, :] = (power / jnp.sum(power, axis=1, keepdims=True)).astype(BF16)

    def pool_chunk(i):
        rows = pl.ds(pl.multiple_of(i * size, size), size)
        assign = own[rows, :]
        over_rows = (((0,), (0,)), ((), ()))
        totals[...] += jnp.dot(jnp.ones((16, size), BF16), assign, preferred_element_type=F32)
        for p in range(4):
            both = jnp.dot(nbuf[rows, :], wbuf[p], preferred_element_type=F32)
            gated = (both[:, :width] * jax.nn.sigmoid(both[:, width:])).astype(BF16)
            pooled[p] += lax.dot_general(assign, gated, over_rows, preferred_element_type=F32)

    def early(i, carry):
        assign_chunk(i)
        return carry

    lax.fori_loop(0, CHUNKS // 2, early, 0)
    w_copy(1).wait_recv()
    w_copy(2).start()
    w_copy(0).wait_recv()
    w_copy(2).wait_recv()

    def late(i, carry):
        assign_chunk(i + CHUNKS // 2)
        pool_chunk(2 * i)
        pool_chunk(2 * i + 1)
        return carry

    lax.fori_loop(0, CHUNKS // 2 - 1, late, 0)
    pool_chunk(CHUNKS - 2)
    assign_chunk(CHUNKS - 1)
    pool_chunk(CHUNKS - 1)

    column = [(far, d) for far in range(2) for d in range(4)][1:]
    held = pooled.shape[1] // 2

    def p_copy(n):
        far, d = column[n]
        return pltpu.make_async_remote_copy(
            src_ref=part_out.at[(z_hi + far) % 2, peers[d]],
            dst_ref=part_in.at[n],
            send_sem=p_send.at[n],
            recv_sem=p_recv.at[n],
            device_id=((slab + far * half) % slabs, peers[d]),
            device_id_type=MESH,
        )

    weights = totals[...]
    for p in range(4):
        for h in range(2):
            part_out[h, p, pl.ds(0, held)] = pooled[p, pl.ds(h * held, held)].astype(BF16)
            part_out[h, p, pl.ds(held, 16), pl.ds(0, 128)] = weights.astype(BF16)
            part_out[h, p, pl.ds(held, 16), pl.ds(128, width - 128)] = jnp.zeros(
                (16, width - 128), BF16
            )
    for n in (1, 2, 3, 4, 5, 6, 0):
        p_copy(n).start()
    for d in (2, 1):
        a_copy(d).start()
    keep = pltpu.make_async_copy(own, assign_ref.at[pl.ds(chan * quarter, quarter)], local_sem.at[0])
    keep.start()
    for n in range(7):
        p_copy(n).wait_recv()
    mine = pooled[chan, pl.ds(pl.multiple_of(z_hi * held, held), held)]
    for n in range(7):
        mine = mine + part_in[n, pl.ds(0, held)].astype(F32)
        weights = weights + part_in[n, pl.ds(held, 16), pl.ds(0, 128)].astype(F32)

    for t in range(half):
        tile_out[t, 0] = mine[8 * (t // 2) : 8 * (t // 2) + 8, 128 * (t % 2) : 128 * (t % 2) + 128]
        tile_out[t, 1] = weights[:8]

    def t_copy(k):
        to = (spot + k) % half
        return pltpu.make_async_remote_copy(
            src_ref=tile_out.at[to],
            dst_ref=tile_in.at[spot],
            send_sem=t_send.at[k - 1],
            recv_sem=t_recv.at[k - 1],
            device_id=(z_hi * half + to, chan),
            device_id_type=MESH,
        )

    def n_copy(k):
        return pltpu.make_async_remote_copy(
            src_ref=new_out,
            dst_ref=new_in.at[slab],
            send_sem=n_send.at[k - 1],
            recv_sem=n_recv.at[k - 1],
            device_id=((slab + k) % slabs, chan),
            device_id_type=MESH,
        )

    def over(number, action):
        def body(k, carry):
            action(k)
            return carry

        lax.fori_loop(1, number, body, 0)

    over(half, lambda k: t_copy(k).start())
    tile_in[spot] = tile_out[spot]
    over(half, lambda k: t_copy(k).wait_recv())
    sums = jnp.sum(tile_in[...], axis=0)
    first = z_hi * held + 8 * (spot // 2)
    row = lax.broadcasted_iota(jnp.int32, (8, 128), 0)
    lane = lax.broadcasted_iota(jnp.int32, (8, 128), 1)
    weight = jnp.sum(jnp.where(lane == row + first, sums[1], 0.0), axis=1, keepdims=True)
    before = latents_ref[
        pl.ds(pl.multiple_of(first, 8), 8), pl.ds(pl.multiple_of(128 * (spot % 2), 128), 128)
    ]
    fresh = before + sums[0] / (weight + 1.0)
    new_out[...] = fresh
    over(slabs, lambda k: n_copy(k).start())
    new_in[slab] = fresh

    def forward():
        rows = pl.ds(peers[2] * quarter, quarter)
        return pltpu.make_async_remote_copy(
            src_ref=assign_ref.at[rows],
            dst_ref=assign_ref.at[rows],
            send_sem=a_send.at[2],
            recv_sem=a_recv.at[2],
            device_id=(slab, peers[1]),
            device_id_type=MESH,
        )

    a_copy(2).wait_recv()
    forward().start()

    over(slabs, lambda k: n_copy(k).wait_recv())
    for t in range(slabs):
        top, left = held * (t // half) + 8 * ((t % half) // 2), 128 * (t % 2)
        latent_ref[top : top + 8, left : left + 128] = new_in[t]

    def drained(i, carry):
        for d in (1, 2, 3):
            x_copy(d, i).wait_send()
        return carry

    lax.fori_loop(0, CHUNKS, drained, 0)
    for which in range(3):
        w_copy(which).wait_send()
    for n in range(7):
        p_copy(n).wait_send()
    over(half, lambda k: t_copy(k).wait_send())
    over(slabs, lambda k: n_copy(k).wait_send())
    a_copy(1).wait_recv()
    for d in (1, 2):
        a_copy(d).wait_send()
    forward().wait()
    keep.wait()


def mix(mixed, weights, keys, gain, latents):
    rows, width = mixed.shape
    slabs = lax.axis_size("slab")
    quarter = rows // 4
    held = latents.shape[0]
    dma = pltpu.SemaphoreType.DMA
    return pl.pallas_call(
        mix_kernel,
        out_shape=(
            jax.ShapeDtypeStruct((rows, held), BF16),
            jax.ShapeDtypeStruct((held, width), F32),
        ),
        in_specs=[
            pl.BlockSpec(memory_space=pl.ANY),
            pl.BlockSpec(memory_space=pl.ANY),
            whole(),
            whole(),
            whole(),
        ],
        out_specs=(pl.BlockSpec(memory_space=pl.ANY), whole()),
        scratch_shapes=[
            pltpu.VMEM((4, quarter, width), BF16),
            pltpu.VMEM((quarter, 4 * width), BF16),
            pltpu.VMEM((4,) + weights.shape, BF16),
            pltpu.VMEM((quarter, held), BF16),
            pltpu.VMEM((4, held, width), F32),
            pltpu.VMEM((16, 128), F32),
            pltpu.VMEM((2, 4, held // 2 + 16, width), BF16),
            pltpu.VMEM((7, held // 2 + 16, width), BF16),
            pltpu.VMEM((slabs // 2, 2, 8, 128), F32),
            pltpu.VMEM((slabs // 2, 2, 8, 128), F32),
            pltpu.VMEM((8, 128), F32),
            pltpu.VMEM((slabs, 8, 128), F32),
            dma((2,)),
            dma((3, CHUNKS)),
            dma((3, CHUNKS)),
            dma((3,)),
            dma((3,)),
            dma((3,)),
            dma((3,)),
            dma((7,)),
            dma((7,)),
            dma((slabs // 2 - 1,)),
            dma((slabs // 2 - 1,)),
            dma((slabs - 1,)),
            dma((slabs - 1,)),
        ],
        compiler_params=pltpu.CompilerParams(
            collective_id=0, has_side_effects=True, vmem_limit_bytes=48 << 20
        ),
        cost_estimate=pl.CostEstimate(flops=10 << 30, bytes_accessed=16 << 20, transcendentals=0),
        name="mix",
    )(mixed, weights, keys, gain, latents)


def per_device(
    tokens,
    refine_feat,
    refine_dest,
    refine_rows,
    conv_w,
    norm_gain,
    w_val,
    w_gate,
    latent_keys,
    latents,
):
    depth, side_y, side_x, width = tokens.shape
    row_count = depth * side_y * side_x
    slabs = lax.axis_size("slab")
    blocks, block_rows = refine_rows.shape
    capacity = max(2, (2 * blocks + slabs - 1) // slabs)
    slots = slabs * capacity

    up = [(i, i + 1) for i in range(slabs - 1)]
    down = [(i + 1, i) for i in range(slabs - 1)]
    before = lax.ppermute(tokens[-1:], "slab", up)
    after = lax.ppermute(tokens[:1], "slab", down)

    sent = pack(refine_dest[:, 0], refine_feat, refine_rows, slabs, capacity, row_count)
    received = lax.all_to_all(
        sent.reshape(slabs, capacity * (block_rows + EXTRA), width),
        "slab",
        split_axis=0,
        concat_axis=0,
        tiled=True,
    )
    received = received.reshape(slots, block_rows + EXTRA, width)

    base = conv(tokens, before, after, conv_w)
    weights = jnp.concatenate([w_val, w_gate], axis=1)

    got = received[:, block_rows, :].astype(jnp.int32)
    rows = got[:, :block_rows] * 128 + got[:, block_rows:]
    grouped = rows.reshape(slots, block_rows // GROUP, GROUP)
    same = grouped[..., :, None] == grouped[..., None, :]
    above = jnp.arange(GROUP)[:, None] < jnp.arange(GROUP)[None, :]
    clash = jnp.any(same & above, axis=(2, 3))
    clash = jnp.concatenate([clash, jnp.any(clash, axis=1, keepdims=True)], axis=1).astype(jnp.int32)

    spots = (rows // 8) * 16 + rows % 8
    mixed = scatter(spots, clash, base, received)
    assign, latent_new = mix(mixed, weights, latent_keys, norm_gain[None, :], latents)
    readback = jnp.dot(assign, latent_new.astype(BF16), preferred_element_type=F32)
    block_out = (mixed.astype(F32) + readback).astype(BF16)
    return (block_out.reshape(depth, side_y, side_x, width), latent_new)


def solution(mesh):
    return jax.shard_map(
        per_device,
        mesh=mesh,
        in_specs=(
            P("slab", None, None, "chan"),
            P("slab", None, "chan"),
            P("slab", None),
            P("slab", None),
            P(None, "chan"),
            P(),
            P(None, "chan"),
            P(None, "chan"),
            P(),
            P(None, "chan"),
        ),
        out_specs=(P("slab", None, None, "chan"), P(None, "chan")),
        check_vma=False,
    )
```

```python
import functools

import jax
import jax.numpy as jnp
from jax import lax
from jax.experimental import pallas as pl
from jax.experimental.pallas import tpu as pltpu
from jax.sharding import PartitionSpec as P


MESH = pl.DeviceIdType.MESH
BF16 = jnp.bfloat16
F32 = jnp.float32
EXTRA = 8


def whole():
    return pl.BlockSpec(memory_space=pltpu.VMEM)


def pack_kernel(capacity, empty, dest_ref, feat_ref, rows_ref, out_ref, taken):
    slots, width = out_ref.shape[0], out_ref.shape[2]
    blocks, rows, _ = feat_ref.shape

    def coded(number):
        both = jnp.concatenate([number // 128, number % 128], axis=1)
        return jnp.broadcast_to(both.astype(F32), (EXTRA, width)).astype(BF16)

    nothing = coded(jnp.full((1, rows), empty, jnp.int32))

    def clear(j, carry):
        out_ref[j, pl.ds(rows, EXTRA), :] = nothing
        return carry

    lax.fori_loop(0, slots, clear, 0)
    for t in range(slots // capacity):
        taken[t] = 0

    def one(b, carry):
        to = dest_ref[b]
        slot = to * capacity + taken[to]
        taken[to] = taken[to] + 1
        out_ref[slot, pl.ds(0, rows), :] = feat_ref[b]
        out_ref[slot, pl.ds(rows, EXTRA), :] = coded(rows_ref[pl.ds(b, 1), :])
        return carry

    lax.fori_loop(0, blocks, one, 0)


def pack(dest, feat, row_ids, slabs, capacity, empty):
    _, rows, width = feat.shape
    slots = slabs * capacity
    return pl.pallas_call(
        functools.partial(pack_kernel, capacity, empty),
        out_shape=jax.ShapeDtypeStruct((slots, rows + EXTRA, width), BF16),
        in_specs=[pl.BlockSpec(memory_space=pltpu.SMEM), whole(), whole()],
        out_specs=whole(),
        scratch_shapes=[pltpu.SMEM((slabs,), jnp.int32)],
        cost_estimate=pl.CostEstimate(flops=0, bytes_accessed=6 << 20, transcendentals=0),
        name="pack",
    )(dest, feat, row_ids)


def conv_kernel(tokens_ref, before_ref, after_ref, w_ref, out_ref, plane):
    z = pl.program_id(0)
    last = pl.num_programs(0) - 1
    _, side_y, side_x, width = tokens_ref.shape

    def widen(slot, value):
        plane[slot, pl.ds(1, side_y)] = value.astype(F32)

    @pl.when(z == 0)
    def _():
        zero = jnp.zeros((side_x, width), F32)
        for slot in range(3):
            plane[slot, 0] = zero
            plane[slot, side_y + 1] = zero
        widen(2, before_ref[0])
        widen(0, tokens_ref[0])

    ahead = lax.rem(z + 1, 3)

    @pl.when(z < last)
    def _():
        widen(ahead, tokens_ref[z + 1])

    @pl.when(z == last)
    def _():
        widen(ahead, after_ref[0])

    slots = (lax.rem(z + 2, 3), lax.rem(z, 3), ahead)
    column = lax.broadcasted_iota(jnp.int32, (side_x, 128), 0)
    for half in range(width // 128):
        lanes = pl.ds(128 * half, 128)

        def one(y, carry):
            sums = [None, None, None]
            for dz in range(3):
                for dy in range(3):
                    row = plane[slots[dz], y + dy, :, lanes]
                    for dx in range(3):
                        k = 9 * dz + 3 * dy + dx
                        term = row * w_ref[pl.ds(k, 1), lanes]
                        sums[dx] = term if sums[dx] is None else sums[dx] + term
            centre = plane[slots[1], y + 1, :, lanes] + sums[1]
            left = jnp.where(column == 0, 0.0, pltpu.roll(sums[0], 1, 0))
            right = jnp.where(column == side_x - 1, 0.0, pltpu.roll(sums[2], side_x - 1, 0))
            value = centre + left + right
            for i in range(0, side_x, 8):
                to = pl.ds(pl.multiple_of(2 * side_x * y + 2 * i + 8 * half, 8), 8)
                out_ref[to, :] = value[i : i + 8]
            return carry

        lax.fori_loop(0, side_y, one, 0)


def conv(tokens, before, after, w):
    depth, side_y, side_x, width = tokens.shape
    rows = side_y * side_x
    fixed = lambda shape: pl.BlockSpec(shape, lambda z: (0,) * len(shape))
    return pl.pallas_call(
        conv_kernel,
        grid=(depth,),
        out_shape=jax.ShapeDtypeStruct((2 * depth * rows, 128), F32),
        in_specs=[fixed(tokens.shape), fixed(before.shape), fixed(after.shape), fixed(w.shape)],
        out_specs=pl.BlockSpec((2 * rows, 128), lambda z: (z, 0)),
        scratch_shapes=[pltpu.VMEM((3, side_y + 2, side_x, width), F32)],
        cost_estimate=pl.CostEstimate(
            flops=54 * depth * rows * width, bytes_accessed=30 << 20, transcendentals=0
        ),
        name="conv",
    )(tokens, before, after, w)


GROUP = 16


def scatter_kernel(
    base_ref,
    recv_ref,
    out_ref,
    acc,
    wide,
    feat,
    codes,
    spots,
    clash,
    out,
    spots_ref,
    clash_ref,
    feat_sems,
    base_sem,
    code_sems,
    out_sems,
):
    slots, block_rows, _ = feat.shape
    total = acc.shape[0] // 2
    pieces = feat_sems.shape[0]
    each = slots // pieces
    step = 128

    code_copy = pltpu.make_async_copy(
        recv_ref.at[pl.ds(0, slots), pl.ds(block_rows, EXTRA)], codes, code_sems.at[0]
    )
    code_copy.start()
    base_copy = pltpu.make_async_copy(base_ref, acc, base_sem)

    def fetch(i):
        return pltpu.make_async_copy(
            recv_ref.at[pl.ds(i * each, each), pl.ds(0, block_rows)],
            feat.at[pl.ds(i * each, each)],
            feat_sems.at[i],
        )

    base_copy.start()
    for i in range(pieces):
        fetch(i).start()

    code_copy.wait()
    code = jnp.max(codes[...].astype(F32), axis=1)
    number = (code[:, :block_rows] * 128.0 + code[:, block_rows:]).astype(jnp.int32)
    spots[...] = (number // 8) * 16 + number % 8
    lane = lax.broadcasted_iota(jnp.int32, number.shape, 1)
    again = jnp.zeros_like(number)
    for k in range(1, GROUP):
        same = (number == pltpu.roll(number, k, 1)) & (lane % GROUP >= k)
        again = jnp.where(same, 1, again)
    k = 1
    while k < GROUP:
        again = jnp.maximum(again, jnp.where(lane % GROUP >= k, pltpu.roll(again, k, 1), 0))
        k *= 2
    most = jnp.max(again.astype(F32), axis=1, keepdims=True).astype(jnp.int32)
    clash[...] = jnp.where(lane == 0, most, again)
    scalars = (
        pltpu.make_async_copy(spots, spots_ref, code_sems.at[1]),
        pltpu.make_async_copy(clash, clash_ref, code_sems.at[2]),
    )
    for copy in scalars:
        copy.start()
    for copy in scalars:
        copy.wait()
    base_copy.wait()

    def at(spot):
        return pl.ds(spot, 2, stride=8)

    def one(j, carry):
        @pl.when(lax.rem(j, each) == 0)
        def _():
            fetch(j // each).wait()

        @pl.when(spots_ref[j, 0] < 2 * total)
        def _():
            for k in range(0, block_rows, 16):
                for h in range(2):
                    value = feat[j, k : k + 16, 128 * h : 128 * h + 128].astype(F32)
                    wide[2 * k + 8 * h : 2 * k + 8 * h + 8, :] = value[:8]
                    wide[2 * k + 16 + 8 * h : 2 * k + 24 + 8 * h, :] = value[8:]

            groups = block_rows // GROUP
            mine = [2 * (c - c % 8) + c % 8 for c in range(block_rows)]

            def together(g):
                places = range(g * GROUP, (g + 1) * GROUP)
                where = [spots_ref[j, c] for c in places]
                news = [acc[at(r), :] + wide[at(mine[c]), :] for r, c in zip(where, places)]
                for r, new in zip(where, news):
                    acc[at(r), :] = new

            @pl.when(clash_ref[j, 0] == 0)
            def _():
                for g in range(groups):
                    together(g)

            @pl.when(clash_ref[j, 0] != 0)
            def _():
                for g in range(groups):

                    @pl.when(clash_ref[j, (g + 1) * GROUP - 1] == 0)
                    def _():
                        together(g)

                    @pl.when(clash_ref[j, (g + 1) * GROUP - 1] != 0)
                    def _():
                        for c in range(g * GROUP, (g + 1) * GROUP):
                            r = spots_ref[j, c]
                            acc[at(r), :] = acc[at(r), :] + wide[at(mine[c]), :]

        return carry

    lax.fori_loop(0, slots, one, 0)

    def finish(i, carry):
        value = acc[pl.ds(pl.multiple_of(i * 2 * step, 2 * step), 2 * step), :]
        value = value.reshape(step // 8, 2, 8, 128)
        part = pl.ds(pl.multiple_of(i * step, step), step)
        for h in range(2):
            out[part, 128 * h : 128 * h + 128] = value[:, h].reshape(step, 128).astype(BF16)
        return carry

    parts = out_sems.shape[0]
    share = total // parts

    def out_copy(p):
        rows = pl.ds(p * share, share)
        return pltpu.make_async_copy(out.at[rows], out_ref.at[rows], out_sems.at[p])

    for p in range(parts):
        lax.fori_loop(p * share // step, (p + 1) * share // step, finish, 0)
        out_copy(p).start()
    for p in range(parts):
        out_copy(p).wait()


def scatter(base, recv):
    total, width = base.shape[0] // 2, 2 * base.shape[1]
    slots, block_rows = recv.shape[0], recv.shape[1] - EXTRA
    anywhere = pl.BlockSpec(memory_space=pl.ANY)
    dma = pltpu.SemaphoreType.DMA
    return pl.pallas_call(
        scatter_kernel,
        out_shape=jax.ShapeDtypeStruct((total, width), BF16),
        in_specs=[anywhere, anywhere],
        out_specs=anywhere,
        scratch_shapes=[
            pltpu.VMEM((2 * total, 128), F32),
            pltpu.VMEM((2 * block_rows, 128), F32),
            pltpu.VMEM((slots, block_rows, width), BF16),
            pltpu.VMEM((slots, EXTRA, width), BF16),
            pltpu.VMEM((slots, block_rows), jnp.int32),
            pltpu.VMEM((slots, block_rows), jnp.int32),
            pltpu.VMEM((total, width), BF16),
            pltpu.SMEM((slots, block_rows), jnp.int32),
            pltpu.SMEM((slots, block_rows), jnp.int32),
            dma((8,)),
            dma,
            dma((3,)),
            dma((4,)),
        ],
        compiler_params=pltpu.CompilerParams(vmem_limit_bytes=60 << 20),
        cost_estimate=pl.CostEstimate(flops=2 << 20, bytes_accessed=16 << 20, transcendentals=0),
        name="scatter",
    )(base, recv)


CHUNKS = 8


def mix_kernel(
    mixed_ref,
    w_ref,
    keys_ref,
    gain_ref,
    latents_ref,
    assign_ref,
    latent_ref,
    xbuf,
    nbuf,
    wbuf,
    own,
    pooled,
    totals,
    part_out,
    part_in,
    tile_out,
    tile_in,
    new_out,
    new_in,
    local_sem,
    x_send,
    x_recv,
    w_send,
    w_recv,
    a_send,
    a_recv,
    p_send,
    p_recv,
    t_send,
    t_recv,
    n_send,
    n_recv,
):
    slab = lax.axis_index("slab")
    chan = lax.axis_index("chan")
    slabs = lax.axis_size("slab")
    z_lo, core = chan // 2, chan % 2
    peers = (
        chan,
        z_lo * 2 + (1 - core),
        (1 - z_lo) * 2 + core,
        (1 - z_lo) * 2 + (1 - core),
    )
    far_slab = (slab + slabs // 2) % slabs
    quarter = xbuf.shape[1]
    size = quarter // CHUNKS
    width = xbuf.shape[2]
    half = slabs // 2
    z_hi, spot = slab // half, slab % half

    def local_copies():
        yield pltpu.make_async_copy(
            mixed_ref.at[pl.ds(chan * quarter, quarter)], xbuf.at[chan], local_sem.at[0]
        )
        yield pltpu.make_async_copy(w_ref, wbuf.at[chan], local_sem.at[1])

    for copy in local_copies():
        copy.start()

    barrier = pltpu.get_barrier_semaphore()
    for d in (1, 2, 3):
        for where in (slab, far_slab):
            pl.semaphore_signal(barrier, inc=1, device_id=(where, peers[d]), device_id_type=MESH)

    pl.semaphore_signal(barrier, inc=1, device_id=(far_slab, chan), device_id_type=MESH)

    def greet(k, carry):
        pl.semaphore_signal(
            barrier,
            inc=1,
            device_id=(z_hi * half + (spot + k) % half, chan),
            device_id_type=MESH,
        )
        return carry

    lax.fori_loop(1, half, greet, 0)
    pl.semaphore_wait(barrier, 7 + half - 1)

    def x_copy(d, i):
        rows = pl.ds(i * size, size)
        return pltpu.make_async_remote_copy(
            src_ref=mixed_ref.at[pl.ds(peers[d] * quarter + i * size, size)],
            dst_ref=xbuf.at[chan, rows],
            send_sem=x_send.at[d - 1, i],
            recv_sem=x_recv.at[d - 1, i],
            device_id=(slab, peers[d]),
            device_id_type=MESH,
        )

    def w_copy(which):
        source, device = (
            (w_ref, (slab, peers[1])),
            (w_ref, (far_slab, peers[2])),
            (wbuf.at[peers[2]], (slab, peers[1])),
        )[which]
        return pltpu.make_async_remote_copy(
            src_ref=source,
            dst_ref=wbuf.at[peers[2] if which == 2 else chan],
            send_sem=w_send.at[which],
            recv_sem=w_recv.at[which],
            device_id=device,
            device_id_type=MESH,
        )

    def a_copy(d):
        return pltpu.make_async_remote_copy(
            src_ref=own,
            dst_ref=assign_ref.at[pl.ds(chan * quarter, quarter)],
            send_sem=a_send.at[d - 1],
            recv_sem=a_recv.at[d - 1],
            device_id=(slab, peers[d]),
            device_id_type=MESH,
        )

    def start_x(i, carry):
        for d in (1, 2, 3):
            x_copy(d, i).start()
        return carry

    w_copy(1).start()
    lax.fori_loop(0, CHUNKS, start_x, 0)
    w_copy(0).start()
    pooled[...] = jnp.zeros_like(pooled)
    totals[...] = jnp.zeros_like(totals)
    for copy in local_copies():
        copy.wait()

    def assign_chunk(i):
        for d in (1, 2, 3):
            x_copy(d, i).wait_recv()
        rows = pl.ds(pl.multiple_of(i * size, size), size)
        wide = [xbuf[p, rows, :].astype(F32) for p in range(4)]
        square = sum(jnp.sum(v * v, axis=1, keepdims=True) for v in wide)
        scale = lax.rsqrt(square * (1.0 / (4 * width)) + 1e-06)
        for p in range(4):
            lanes = pl.ds(p * width, width)
            nbuf[rows, lanes] = (wide[p] * scale * gain_ref[:, lanes]).astype(BF16)
        scores = lax.dot_general(
            nbuf[rows, :], keys_ref[...], (((1,), (1,)), ((), ())), preferred_element_type=F32
        )
        scores = scores * (4 * width) ** (-0.5)
        top = jnp.max(scores, axis=1, keepdims=True)
        power = jnp.exp(scores - top)
        own[rows, :] = (power / jnp.sum(power, axis=1, keepdims=True)).astype(BF16)

    def pool_chunk(i):
        rows = pl.ds(pl.multiple_of(i * size, size), size)
        assign = own[rows, :]
        over_rows = (((0,), (0,)), ((), ()))
        totals[...] += jnp.dot(jnp.ones((16, size), BF16), assign, preferred_element_type=F32)
        for p in range(4):
            both = jnp.dot(nbuf[rows, :], wbuf[p], preferred_element_type=F32)
            gated = (both[:, :width] * jax.nn.sigmoid(both[:, width:])).astype(BF16)
            pooled[p] += lax.dot_general(assign, gated, over_rows, preferred_element_type=F32)

    def early(i, carry):
        assign_chunk(i)
        return carry

    lax.fori_loop(0, CHUNKS // 2, early, 0)
    w_copy(1).wait_recv()
    w_copy(2).start()
    w_copy(0).wait_recv()
    w_copy(2).wait_recv()

    def late(i, carry):
        assign_chunk(i + CHUNKS // 2)
        pool_chunk(2 * i)
        pool_chunk(2 * i + 1)
        return carry

    lax.fori_loop(0, CHUNKS // 2 - 1, late, 0)
    pool_chunk(CHUNKS - 2)
    assign_chunk(CHUNKS - 1)
    pool_chunk(CHUNKS - 1)

    column = [(far, d) for far in range(2) for d in range(4)][1:]
    held = pooled.shape[1]
    place = z_hi * 4 + chan

    def p_copy(n):
        far, d = column[n]
        return pltpu.make_async_remote_copy(
            src_ref=part_out.at[peers[d]],
            dst_ref=part_in.at[place],
            send_sem=p_send.at[n],
            recv_sem=p_recv.at[n],
            device_id=((slab + far * half) % slabs, peers[d]),
            device_id_type=MESH,
        )

    weights = totals[...].astype(BF16)
    for p in range(4):
        part_out[p, pl.ds(0, held)] = pooled[p].astype(BF16)
        part_out[p, pl.ds(held, 16), pl.ds(0, 128)] = weights
        part_out[p, pl.ds(held, 16), pl.ds(128, width - 128)] = jnp.zeros((16, width - 128), BF16)
    for n in (4, 1, 2, 5, 6, 3, 0):
        p_copy(n).start()
    for d in (2, 1):
        a_copy(d).start()
    keep = pltpu.make_async_copy(own, assign_ref.at[pl.ds(chan * quarter, quarter)], local_sem.at[0])
    keep.start()
    part_in[place] = part_out[chan]
    for n in range(7):
        p_copy(n).wait_recv()
    mine = part_in[0, pl.ds(0, held)].astype(F32)
    total = part_in[0, pl.ds(held, 16), pl.ds(0, 128)].astype(F32)
    for n in range(1, 8):
        mine = mine + part_in[n, pl.ds(0, held)].astype(F32)
        total = total + part_in[n, pl.ds(held, 16), pl.ds(0, 128)].astype(F32)

    for t in range(half):
        for h in range(2):
            tile_out[t, h] = mine[8 * t : 8 * t + 8, 128 * h : 128 * h + 128]
        tile_out[t, 2] = total[:8]

    def plane_copy(k, source, target, send, recv):
        return pltpu.make_async_remote_copy(
            src_ref=source,
            dst_ref=target.at[spot],
            send_sem=send.at[k - 1],
            recv_sem=recv.at[k - 1],
            device_id=(z_hi * half + (spot + k) % half, chan),
            device_id_type=MESH,
        )

    def t_copy(k):
        return plane_copy(k, tile_out.at[(spot + k) % half], tile_in, t_send, t_recv)

    def n_copy(k):
        return plane_copy(k, new_out, new_in, n_send, n_recv)

    def over(number, action):
        def body(k, carry):
            action(k)
            return carry

        lax.fori_loop(1, number, body, 0)

    over(half, lambda k: t_copy(k).start())
    tile_in[spot] = tile_out[spot]
    over(half, lambda k: t_copy(k).wait_recv())
    sums = jnp.sum(tile_in[...], axis=0)
    first = 8 * spot
    row = lax.broadcasted_iota(jnp.int32, (8, 128), 0)
    lane = lax.broadcasted_iota(jnp.int32, (8, 128), 1)
    weight = jnp.sum(jnp.where(lane == row + first, sums[2], 0.0), axis=1, keepdims=True)
    for h in range(2):
        before = latents_ref[
            pl.ds(pl.multiple_of(first, 8), 8), pl.ds(128 * h, 128)
        ]
        new_out[h] = before + sums[h] / (weight + 1.0)
    over(half, lambda k: n_copy(k).start())
    new_in[spot] = new_out[...]

    def forward():
        rows = pl.ds(peers[2] * quarter, quarter)
        return pltpu.make_async_remote_copy(
            src_ref=assign_ref.at[rows],
            dst_ref=assign_ref.at[rows],
            send_sem=a_send.at[2],
            recv_sem=a_recv.at[2],
            device_id=(slab, peers[1]),
            device_id_type=MESH,
        )

    a_copy(2).wait_recv()
    forward().start()

    over(half, lambda k: n_copy(k).wait_recv())
    for t in range(half):
        for h in range(2):
            latent_ref[8 * t : 8 * t + 8, 128 * h : 128 * h + 128] = new_in[t, h]

    def drained(i, carry):
        for d in (1, 2, 3):
            x_copy(d, i).wait_send()
        return carry

    lax.fori_loop(0, CHUNKS, drained, 0)
    for which in range(3):
        w_copy(which).wait_send()
    for n in range(7):
        p_copy(n).wait_send()
    over(half, lambda k: t_copy(k).wait_send())
    over(half, lambda k: n_copy(k).wait_send())
    a_copy(1).wait_recv()
    for d in (1, 2):
        a_copy(d).wait_send()
    forward().wait()
    keep.wait()


def mix(mixed, weights, keys, gain, latents):
    rows, width = mixed.shape
    slabs = lax.axis_size("slab")
    quarter = rows // 4
    held = latents.shape[0]
    dma = pltpu.SemaphoreType.DMA
    return pl.pallas_call(
        mix_kernel,
        out_shape=(
            jax.ShapeDtypeStruct((rows, held), BF16),
            jax.ShapeDtypeStruct((held, width), F32),
        ),
        in_specs=[
            pl.BlockSpec(memory_space=pl.ANY),
            pl.BlockSpec(memory_space=pl.ANY),
            whole(),
            whole(),
            whole(),
        ],
        out_specs=(pl.BlockSpec(memory_space=pl.ANY), whole()),
        scratch_shapes=[
            pltpu.VMEM((4, quarter, width), BF16),
            pltpu.VMEM((quarter, 4 * width), BF16),
            pltpu.VMEM((4,) + weights.shape, BF16),
            pltpu.VMEM((quarter, held), BF16),
            pltpu.VMEM((4, held, width), F32),
            pltpu.VMEM((16, 128), F32),
            pltpu.VMEM((4, held + 16, width), BF16),
            pltpu.VMEM((8, held + 16, width), BF16),
            pltpu.VMEM((slabs // 2, 3, 8, 128), F32),
            pltpu.VMEM((slabs // 2, 3, 8, 128), F32),
            pltpu.VMEM((2, 8, 128), F32),
            pltpu.VMEM((slabs // 2, 2, 8, 128), F32),
            dma((2,)),
            dma((3, CHUNKS)),
            dma((3, CHUNKS)),
            dma((3,)),
            dma((3,)),
            dma((3,)),
            dma((3,)),
            dma((7,)),
            dma((7,)),
            dma((slabs // 2 - 1,)),
            dma((slabs // 2 - 1,)),
            dma((slabs // 2 - 1,)),
            dma((slabs // 2 - 1,)),
        ],
        compiler_params=pltpu.CompilerParams(
            collective_id=0, has_side_effects=True, vmem_limit_bytes=48 << 20
        ),
        cost_estimate=pl.CostEstimate(flops=10 << 30, bytes_accessed=16 << 20, transcendentals=0),
        name="mix",
    )(mixed, weights, keys, gain, latents)


def per_device(
    tokens,
    refine_feat,
    refine_dest,
    refine_rows,
    conv_w,
    norm_gain,
    w_val,
    w_gate,
    latent_keys,
    latents,
):
    depth, side_y, side_x, width = tokens.shape
    row_count = depth * side_y * side_x
    slabs = lax.axis_size("slab")
    blocks, block_rows = refine_rows.shape
    capacity = max(2, (2 * blocks + slabs - 1) // slabs)
    slots = slabs * capacity

    up = [(i, i + 1) for i in range(slabs - 1)]
    down = [(i + 1, i) for i in range(slabs - 1)]
    before = lax.ppermute(tokens[-1:], "slab", up)
    after = lax.ppermute(tokens[:1], "slab", down)

    sent = pack(refine_dest[:, 0], refine_feat, refine_rows, slabs, capacity, row_count)
    received = lax.all_to_all(
        sent.reshape(slabs, capacity * (block_rows + EXTRA), width),
        "slab",
        split_axis=0,
        concat_axis=0,
        tiled=True,
    )
    received = received.reshape(slots, block_rows + EXTRA, width)

    base = conv(tokens, before, after, conv_w)
    weights = jnp.concatenate([w_val, w_gate], axis=1)

    mixed = scatter(base, received)
    assign, latent_new = mix(mixed, weights, latent_keys, norm_gain[None, :], latents)
    readback = jnp.dot(assign, latent_new.astype(BF16), preferred_element_type=F32)
    block_out = (mixed.astype(F32) + readback).astype(BF16)
    return (block_out.reshape(depth, side_y, side_x, width), latent_new)


def solution(mesh):
    return jax.shard_map(
        per_device,
        mesh=mesh,
        in_specs=(
            P("slab", None, None, "chan"),
            P("slab", None, "chan"),
            P("slab", None),
            P("slab", None),
            P(None, "chan"),
            P(),
            P(None, "chan"),
            P(None, "chan"),
            P(),
            P(None, "chan"),
        ),
        out_specs=(P("slab", None, None, "chan"), P(None, "chan")),
        check_vma=False,
    )
```

```python
import functools

import jax
import jax.numpy as jnp
from jax import lax
from jax.experimental import pallas as pl
from jax.experimental.pallas import tpu as pltpu
from jax.sharding import PartitionSpec as P


MESH = pl.DeviceIdType.MESH
BF16 = jnp.bfloat16
F32 = jnp.float32
EXTRA = 8


def whole():
    return pl.BlockSpec(memory_space=pltpu.VMEM)


def pack_kernel(
    capacity, empty, dest_ref, feat_ref, rows_ref, out_ref, taken, slot_of, feat, codes, in_sems, out_sems, code_sem
):
    slots, _, width = out_ref.shape
    blocks, rows, _ = feat_ref.shape
    pieces = in_sems.shape[0]
    each = blocks // pieces

    def fetch(i):
        part = pl.ds(i * each, each)
        return pltpu.make_async_copy(feat_ref.at[part], feat.at[part], in_sems.at[i])

    for i in range(pieces):
        fetch(i).start()

    def coded(number):
        both = jnp.concatenate([number // 128, number % 128], axis=1)
        return jnp.broadcast_to(both.astype(F32), (EXTRA, width)).astype(BF16)

    nothing = coded(jnp.full((1, rows), empty, jnp.int32))

    def clear(j, carry):
        codes[j] = nothing
        return carry

    lax.fori_loop(0, slots, clear, 0)
    for t in range(slots // capacity):
        taken[t] = 0

    def place(b, carry):
        to = dest_ref[b]
        slot = to * capacity + taken[to]
        taken[to] = taken[to] + 1
        slot_of[b] = slot
        codes[slot] = coded(rows_ref[pl.ds(b, 1), :])
        return carry

    lax.fori_loop(0, blocks, place, 0)
    code_copy = pltpu.make_async_copy(
        codes, out_ref.at[pl.ds(0, slots), pl.ds(rows, EXTRA)], code_sem
    )
    code_copy.start()

    def put(b):
        return pltpu.make_async_copy(
            feat.at[b], out_ref.at[slot_of[b], pl.ds(0, rows)], out_sems.at[b]
        )

    def send(b, carry):
        put(b).start()
        return carry

    def finish(b, carry):
        put(b).wait()
        return carry

    for i in range(pieces):
        fetch(i).wait()
        lax.fori_loop(i * each, (i + 1) * each, send, 0)
    lax.fori_loop(0, blocks, finish, 0)
    code_copy.wait()


def pack(dest, feat, row_ids, slabs, capacity, empty):
    blocks, rows, width = feat.shape
    slots = slabs * capacity
    anywhere = pl.BlockSpec(memory_space=pl.ANY)
    dma = pltpu.SemaphoreType.DMA
    return pl.pallas_call(
        functools.partial(pack_kernel, capacity, empty),
        out_shape=jax.ShapeDtypeStruct((slots, rows + EXTRA, width), BF16),
        in_specs=[pl.BlockSpec(memory_space=pltpu.SMEM), anywhere, whole()],
        out_specs=anywhere,
        scratch_shapes=[
            pltpu.SMEM((slabs,), jnp.int32),
            pltpu.SMEM((blocks,), jnp.int32),
            pltpu.VMEM(feat.shape, BF16),
            pltpu.VMEM((slots, EXTRA, width), BF16),
            dma((4,)),
            dma((blocks,)),
            dma,
        ],
        compiler_params=pltpu.CompilerParams(vmem_limit_bytes=60 << 20),
        cost_estimate=pl.CostEstimate(flops=0, bytes_accessed=6 << 20, transcendentals=0),
        name="pack",
    )(dest, feat, row_ids)


def conv_kernel(tokens_ref, before_ref, after_ref, w_ref, out_ref, plane):
    z = pl.program_id(0)
    last = pl.num_programs(0) - 1
    _, side_y, side_x, width = tokens_ref.shape

    def widen(slot, value):
        plane[slot, pl.ds(1, side_y)] = value.astype(F32)

    @pl.when(z == 0)
    def _():
        zero = jnp.zeros((side_x, width), F32)
        for slot in range(3):
            plane[slot, 0] = zero
            plane[slot, side_y + 1] = zero
        widen(2, before_ref[0])
        widen(0, tokens_ref[0])

    ahead = lax.rem(z + 1, 3)

    @pl.when(z < last)
    def _():
        widen(ahead, tokens_ref[z + 1])

    @pl.when(z == last)
    def _():
        widen(ahead, after_ref[0])

    slots = (lax.rem(z + 2, 3), lax.rem(z, 3), ahead)
    column = lax.broadcasted_iota(jnp.int32, (side_x, 128), 0)
    for half in range(width // 128):
        lanes = pl.ds(128 * half, 128)

        def one(y, carry):
            sums = [None, None, None]
            for dz in range(3):
                for dy in range(3):
                    row = plane[slots[dz], y + dy, :, lanes]
                    for dx in range(3):
                        k = 9 * dz + 3 * dy + dx
                        term = row * w_ref[pl.ds(k, 1), lanes]
                        sums[dx] = term if sums[dx] is None else sums[dx] + term
            centre = plane[slots[1], y + 1, :, lanes] + sums[1]
            left = jnp.where(column == 0, 0.0, pltpu.roll(sums[0], 1, 0))
            right = jnp.where(column == side_x - 1, 0.0, pltpu.roll(sums[2], side_x - 1, 0))
            value = centre + left + right
            for i in range(0, side_x, 8):
                to = pl.ds(pl.multiple_of(2 * side_x * y + 2 * i + 8 * half, 8), 8)
                out_ref[to, :] = value[i : i + 8]
            return carry

        lax.fori_loop(0, side_y, one, 0)


def conv(tokens, before, after, w):
    depth, side_y, side_x, width = tokens.shape
    rows = side_y * side_x
    fixed = lambda shape: pl.BlockSpec(shape, lambda z: (0,) * len(shape))
    return pl.pallas_call(
        conv_kernel,
        grid=(depth,),
        out_shape=jax.ShapeDtypeStruct((2 * depth * rows, 128), F32),
        in_specs=[fixed(tokens.shape), fixed(before.shape), fixed(after.shape), fixed(w.shape)],
        out_specs=pl.BlockSpec((2 * rows, 128), lambda z: (z, 0)),
        scratch_shapes=[pltpu.VMEM((3, side_y + 2, side_x, width), F32)],
        cost_estimate=pl.CostEstimate(
            flops=54 * depth * rows * width, bytes_accessed=30 << 20, transcendentals=0
        ),
        name="conv",
    )(tokens, before, after, w)


GROUP = 16


def scatter_kernel(
    base_ref,
    recv_ref,
    out_ref,
    acc,
    wide,
    feat,
    codes,
    spots,
    clash,
    out,
    spots_ref,
    clash_ref,
    feat_sems,
    base_sem,
    code_sems,
    out_sems,
):
    slots, block_rows, _ = feat.shape
    total = acc.shape[0] // 2
    pieces = feat_sems.shape[0]
    each = slots // pieces
    step = 128

    code_copy = pltpu.make_async_copy(
        recv_ref.at[pl.ds(0, slots), pl.ds(block_rows, EXTRA)], codes, code_sems.at[0]
    )
    code_copy.start()
    base_copy = pltpu.make_async_copy(base_ref, acc, base_sem)

    def fetch(i):
        return pltpu.make_async_copy(
            recv_ref.at[pl.ds(i * each, each), pl.ds(0, block_rows)],
            feat.at[pl.ds(i * each, each)],
            feat_sems.at[i],
        )

    base_copy.start()
    for i in range(pieces):
        fetch(i).start()

    code_copy.wait()
    code = jnp.max(codes[...].astype(F32), axis=1)
    number = (code[:, :block_rows] * 128.0 + code[:, block_rows:]).astype(jnp.int32)
    spots[...] = (number // 8) * 16 + number % 8
    lane = lax.broadcasted_iota(jnp.int32, number.shape, 1)
    again = jnp.zeros_like(number)
    for k in range(1, GROUP):
        same = (number == pltpu.roll(number, k, 1)) & (lane % GROUP >= k)
        again = jnp.where(same, 1, again)
    k = 1
    while k < GROUP:
        again = jnp.maximum(again, jnp.where(lane % GROUP >= k, pltpu.roll(again, k, 1), 0))
        k *= 2
    most = jnp.max(again.astype(F32), axis=1, keepdims=True).astype(jnp.int32)
    clash[...] = jnp.where(lane == 0, most, again)
    scalars = (
        pltpu.make_async_copy(spots, spots_ref, code_sems.at[1]),
        pltpu.make_async_copy(clash, clash_ref, code_sems.at[2]),
    )
    for copy in scalars:
        copy.start()
    for copy in scalars:
        copy.wait()
    base_copy.wait()

    def at(spot):
        return pl.ds(spot, 2, stride=8)

    def one(j, carry):
        @pl.when(lax.rem(j, each) == 0)
        def _():
            fetch(j // each).wait()

        @pl.when(spots_ref[j, 0] < 2 * total)
        def _():
            for k in range(0, block_rows, 16):
                for h in range(2):
                    value = feat[j, k : k + 16, 128 * h : 128 * h + 128].astype(F32)
                    wide[2 * k + 8 * h : 2 * k + 8 * h + 8, :] = value[:8]
                    wide[2 * k + 16 + 8 * h : 2 * k + 24 + 8 * h, :] = value[8:]

            groups = block_rows // GROUP
            mine = [2 * (c - c % 8) + c % 8 for c in range(block_rows)]

            def together(g):
                places = range(g * GROUP, (g + 1) * GROUP)
                where = [spots_ref[j, c] for c in places]
                news = [acc[at(r), :] + wide[at(mine[c]), :] for r, c in zip(where, places)]
                for r, new in zip(where, news):
                    acc[at(r), :] = new

            @pl.when(clash_ref[j, 0] == 0)
            def _():
                for g in range(groups):
                    together(g)

            @pl.when(clash_ref[j, 0] != 0)
            def _():
                for g in range(groups):

                    @pl.when(clash_ref[j, (g + 1) * GROUP - 1] == 0)
                    def _():
                        together(g)

                    @pl.when(clash_ref[j, (g + 1) * GROUP - 1] != 0)
                    def _():
                        for c in range(g * GROUP, (g + 1) * GROUP):
                            r = spots_ref[j, c]
                            acc[at(r), :] = acc[at(r), :] + wide[at(mine[c]), :]

        return carry

    lax.fori_loop(0, slots, one, 0)

    def finish(i, carry):
        value = acc[pl.ds(pl.multiple_of(i * 2 * step, 2 * step), 2 * step), :]
        value = value.reshape(step // 8, 2, 8, 128)
        part = pl.ds(pl.multiple_of(i * step, step), step)
        for h in range(2):
            out[part, 128 * h : 128 * h + 128] = value[:, h].reshape(step, 128).astype(BF16)
        return carry

    parts = out_sems.shape[0]
    share = total // parts

    def out_copy(p):
        rows = pl.ds(p * share, share)
        return pltpu.make_async_copy(out.at[rows], out_ref.at[rows], out_sems.at[p])

    for p in range(parts):
        lax.fori_loop(p * share // step, (p + 1) * share // step, finish, 0)
        out_copy(p).start()
    for p in range(parts):
        out_copy(p).wait()


def scatter(base, recv):
    total, width = base.shape[0] // 2, 2 * base.shape[1]
    slots, block_rows = recv.shape[0], recv.shape[1] - EXTRA
    anywhere = pl.BlockSpec(memory_space=pl.ANY)
    dma = pltpu.SemaphoreType.DMA
    return pl.pallas_call(
        scatter_kernel,
        out_shape=jax.ShapeDtypeStruct((total, width), BF16),
        in_specs=[anywhere, anywhere],
        out_specs=anywhere,
        scratch_shapes=[
            pltpu.VMEM((2 * total, 128), F32),
            pltpu.VMEM((2 * block_rows, 128), F32),
            pltpu.VMEM((slots, block_rows, width), BF16),
            pltpu.VMEM((slots, EXTRA, width), BF16),
            pltpu.VMEM((slots, block_rows), jnp.int32),
            pltpu.VMEM((slots, block_rows), jnp.int32),
            pltpu.VMEM((total, width), BF16),
            pltpu.SMEM((slots, block_rows), jnp.int32),
            pltpu.SMEM((slots, block_rows), jnp.int32),
            dma((8,)),
            dma,
            dma((3,)),
            dma((4,)),
        ],
        compiler_params=pltpu.CompilerParams(vmem_limit_bytes=60 << 20),
        cost_estimate=pl.CostEstimate(flops=2 << 20, bytes_accessed=16 << 20, transcendentals=0),
        name="scatter",
    )(base, recv)


CHUNKS = 8


def mix_kernel(
    mixed_ref,
    w_ref,
    keys_ref,
    gain_ref,
    latents_ref,
    assign_ref,
    latent_ref,
    xbuf,
    nbuf,
    wbuf,
    own,
    pooled,
    totals,
    part_out,
    part_in,
    tile_out,
    tile_in,
    new_out,
    new_in,
    local_sem,
    x_send,
    x_recv,
    w_send,
    w_recv,
    a_send,
    a_recv,
    p_send,
    p_recv,
    t_send,
    t_recv,
    n_send,
    n_recv,
):
    slab = lax.axis_index("slab")
    chan = lax.axis_index("chan")
    slabs = lax.axis_size("slab")
    z_lo, core = chan // 2, chan % 2
    peers = (
        chan,
        z_lo * 2 + (1 - core),
        (1 - z_lo) * 2 + core,
        (1 - z_lo) * 2 + (1 - core),
    )
    far_slab = (slab + slabs // 2) % slabs
    quarter = xbuf.shape[1]
    size = quarter // CHUNKS
    width = xbuf.shape[2]
    half = slabs // 2
    z_hi, spot = slab // half, slab % half

    def local_copies():
        yield pltpu.make_async_copy(
            mixed_ref.at[pl.ds(chan * quarter, quarter)], xbuf.at[chan], local_sem.at[0]
        )
        yield pltpu.make_async_copy(w_ref, wbuf.at[chan], local_sem.at[1])

    for copy in local_copies():
        copy.start()

    barrier = pltpu.get_barrier_semaphore()
    for d in (1, 2, 3):
        for where in (slab, far_slab):
            pl.semaphore_signal(barrier, inc=1, device_id=(where, peers[d]), device_id_type=MESH)

    pl.semaphore_signal(barrier, inc=1, device_id=(far_slab, chan), device_id_type=MESH)

    def greet(k, carry):
        pl.semaphore_signal(
            barrier,
            inc=1,
            device_id=(z_hi * half + (spot + k) % half, chan),
            device_id_type=MESH,
        )
        return carry

    lax.fori_loop(1, half, greet, 0)
    pl.semaphore_wait(barrier, 7 + half - 1)

    def x_copy(d, i):
        rows = pl.ds(i * size, size)
        return pltpu.make_async_remote_copy(
            src_ref=mixed_ref.at[pl.ds(peers[d] * quarter + i * size, size)],
            dst_ref=xbuf.at[chan, rows],
            send_sem=x_send.at[d - 1, i],
            recv_sem=x_recv.at[d - 1, i],
            device_id=(slab, peers[d]),
            device_id_type=MESH,
        )

    def w_copy(which):
        source, device = (
            (w_ref, (slab, peers[1])),
            (w_ref, (far_slab, peers[2])),
            (wbuf.at[peers[2]], (slab, peers[1])),
        )[which]
        return pltpu.make_async_remote_copy(
            src_ref=source,
            dst_ref=wbuf.at[peers[2] if which == 2 else chan],
            send_sem=w_send.at[which],
            recv_sem=w_recv.at[which],
            device_id=device,
            device_id_type=MESH,
        )

    part_rows = quarter // 2

    def a_copy(d, i):
        return pltpu.make_async_remote_copy(
            src_ref=own.at[pl.ds(i * part_rows, part_rows)],
            dst_ref=assign_ref.at[pl.ds(chan * quarter + i * part_rows, part_rows)],
            send_sem=a_send.at[d - 1, i],
            recv_sem=a_recv.at[d - 1, i],
            device_id=(slab, peers[d]),
            device_id_type=MESH,
        )

    def start_x(i, carry):
        for d in (1, 2, 3):
            x_copy(d, i).start()
        return carry

    w_copy(1).start()
    lax.fori_loop(0, CHUNKS, start_x, 0)
    w_copy(0).start()
    pooled[...] = jnp.zeros_like(pooled)
    totals[...] = jnp.zeros_like(totals)
    for copy in local_copies():
        copy.wait()

    def assign_chunk(i):
        for d in (1, 2, 3):
            x_copy(d, i).wait_recv()
        rows = pl.ds(pl.multiple_of(i * size, size), size)
        wide = [xbuf[p, rows, :].astype(F32) for p in range(4)]
        square = sum(jnp.sum(v * v, axis=1, keepdims=True) for v in wide)
        scale = lax.rsqrt(square * (1.0 / (4 * width)) + 1e-06)
        for p in range(4):
            lanes = pl.ds(p * width, width)
            nbuf[rows, lanes] = (wide[p] * scale * gain_ref[:, lanes]).astype(BF16)
        scores = lax.dot_general(
            nbuf[rows, :], keys_ref[...], (((1,), (1,)), ((), ())), preferred_element_type=F32
        )
        scores = scores * (4 * width) ** (-0.5)
        top = jnp.max(scores, axis=1, keepdims=True)
        power = jnp.exp(scores - top)
        own[rows, :] = (power / jnp.sum(power, axis=1, keepdims=True)).astype(BF16)

    def pool_chunk(i):
        rows = pl.ds(pl.multiple_of(i * size, size), size)
        assign = own[rows, :]
        over_rows = (((0,), (0,)), ((), ()))
        totals[...] += jnp.dot(jnp.ones((16, size), BF16), assign, preferred_element_type=F32)
        for p in range(4):
            both = jnp.dot(nbuf[rows, :], wbuf[p], preferred_element_type=F32)
            gated = (both[:, :width] * jax.nn.sigmoid(both[:, width:])).astype(BF16)
            pooled[p] += lax.dot_general(assign, gated, over_rows, preferred_element_type=F32)

    def early(i, carry):
        assign_chunk(i)
        return carry

    lax.fori_loop(0, CHUNKS // 2, early, 0)
    w_copy(1).wait_recv()
    w_copy(2).start()
    w_copy(0).wait_recv()
    w_copy(2).wait_recv()

    def late(i, carry):
        assign_chunk(i + CHUNKS // 2)
        pool_chunk(2 * i)
        pool_chunk(2 * i + 1)
        return carry

    lax.fori_loop(0, CHUNKS // 2 - 1, late, 0)
    pool_chunk(CHUNKS - 2)
    assign_chunk(CHUNKS - 1)
    pool_chunk(CHUNKS - 1)

    column = [(far, d) for far in range(2) for d in range(4)][1:]
    held = pooled.shape[1]
    place = z_hi * 4 + chan

    def p_copy(n):
        far, d = column[n]
        return pltpu.make_async_remote_copy(
            src_ref=part_out.at[peers[d]],
            dst_ref=part_in.at[place],
            send_sem=p_send.at[n],
            recv_sem=p_recv.at[n],
            device_id=((slab + far * half) % slabs, peers[d]),
            device_id_type=MESH,
        )

    weights = totals[...].astype(BF16)
    for p in range(4):
        part_out[p, pl.ds(0, held)] = pooled[p].astype(BF16)
        part_out[p, pl.ds(held, 16), pl.ds(0, 128)] = weights
        part_out[p, pl.ds(held, 16), pl.ds(128, width - 128)] = jnp.zeros((16, width - 128), BF16)
    for n in (4, 1, 2, 5, 6, 3, 0):
        p_copy(n).start()
    for i in range(2):
        for d in (2, 1):
            a_copy(d, i).start()
    keep = pltpu.make_async_copy(own, assign_ref.at[pl.ds(chan * quarter, quarter)], local_sem.at[0])
    keep.start()
    part_in[place] = part_out[chan]
    for n in range(7):
        p_copy(n).wait_recv()
    mine = part_in[0, pl.ds(0, held)].astype(F32)
    total = part_in[0, pl.ds(held, 16), pl.ds(0, 128)].astype(F32)
    for n in range(1, 8):
        mine = mine + part_in[n, pl.ds(0, held)].astype(F32)
        total = total + part_in[n, pl.ds(held, 16), pl.ds(0, 128)].astype(F32)

    for t in range(half):
        for h in range(2):
            tile_out[t, h] = mine[8 * t : 8 * t + 8, 128 * h : 128 * h + 128]
        tile_out[t, 2] = total[:8]

    def plane_copy(k, source, target, send, recv):
        return pltpu.make_async_remote_copy(
            src_ref=source,
            dst_ref=target.at[spot],
            send_sem=send.at[k - 1],
            recv_sem=recv.at[k - 1],
            device_id=(z_hi * half + (spot + k) % half, chan),
            device_id_type=MESH,
        )

    def t_copy(k):
        return plane_copy(k, tile_out.at[(spot + k) % half], tile_in, t_send, t_recv)

    def n_copy(k):
        return plane_copy(k, new_out, new_in, n_send, n_recv)

    def over(number, action):
        def body(k, carry):
            action(k)
            return carry

        lax.fori_loop(1, number, body, 0)

    over(half, lambda k: t_copy(k).start())
    tile_in[spot] = tile_out[spot]
    over(half, lambda k: t_copy(k).wait_recv())
    sums = jnp.sum(tile_in[...], axis=0)
    first = 8 * spot
    row = lax.broadcasted_iota(jnp.int32, (8, 128), 0)
    lane = lax.broadcasted_iota(jnp.int32, (8, 128), 1)
    weight = jnp.sum(jnp.where(lane == row + first, sums[2], 0.0), axis=1, keepdims=True)
    for h in range(2):
        before = latents_ref[
            pl.ds(pl.multiple_of(first, 8), 8), pl.ds(128 * h, 128)
        ]
        new_out[h] = before + sums[h] / (weight + 1.0)
    over(half, lambda k: n_copy(k).start())
    new_in[spot] = new_out[...]

    def forward(i):
        rows = pl.ds(peers[2] * quarter + i * part_rows, part_rows)
        return pltpu.make_async_remote_copy(
            src_ref=assign_ref.at[rows],
            dst_ref=assign_ref.at[rows],
            send_sem=a_send.at[2, i],
            recv_sem=a_recv.at[2, i],
            device_id=(slab, peers[1]),
            device_id_type=MESH,
        )

    for i in range(2):
        a_copy(2, i).wait_recv()
        forward(i).start()

    over(half, lambda k: n_copy(k).wait_recv())
    for t in range(half):
        for h in range(2):
            latent_ref[8 * t : 8 * t + 8, 128 * h : 128 * h + 128] = new_in[t, h]

    def drained(i, carry):
        for d in (1, 2, 3):
            x_copy(d, i).wait_send()
        return carry

    lax.fori_loop(0, CHUNKS, drained, 0)
    for which in range(3):
        w_copy(which).wait_send()
    for n in range(7):
        p_copy(n).wait_send()
    over(half, lambda k: t_copy(k).wait_send())
    over(half, lambda k: n_copy(k).wait_send())
    for i in range(2):
        a_copy(1, i).wait_recv()
        for d in (1, 2):
            a_copy(d, i).wait_send()
        forward(i).wait()
    keep.wait()


def mix(mixed, weights, keys, gain, latents):
    rows, width = mixed.shape
    slabs = lax.axis_size("slab")
    quarter = rows // 4
    held = latents.shape[0]
    dma = pltpu.SemaphoreType.DMA
    return pl.pallas_call(
        mix_kernel,
        out_shape=(
            jax.ShapeDtypeStruct((rows, held), BF16),
            jax.ShapeDtypeStruct((held, width), F32),
        ),
        in_specs=[
            pl.BlockSpec(memory_space=pl.ANY),
            pl.BlockSpec(memory_space=pl.ANY),
            whole(),
            whole(),
            whole(),
        ],
        out_specs=(pl.BlockSpec(memory_space=pl.ANY), whole()),
        scratch_shapes=[
            pltpu.VMEM((4, quarter, width), BF16),
            pltpu.VMEM((quarter, 4 * width), BF16),
            pltpu.VMEM((4,) + weights.shape, BF16),
            pltpu.VMEM((quarter, held), BF16),
            pltpu.VMEM((4, held, width), F32),
            pltpu.VMEM((16, 128), F32),
            pltpu.VMEM((4, held + 16, width), BF16),
            pltpu.VMEM((8, held + 16, width), BF16),
            pltpu.VMEM((slabs // 2, 3, 8, 128), F32),
            pltpu.VMEM((slabs // 2, 3, 8, 128), F32),
            pltpu.VMEM((2, 8, 128), F32),
            pltpu.VMEM((slabs // 2, 2, 8, 128), F32),
            dma((2,)),
            dma((3, CHUNKS)),
            dma((3, CHUNKS)),
            dma((3,)),
            dma((3,)),
            dma((3, 2)),
            dma((3, 2)),
            dma((7,)),
            dma((7,)),
            dma((slabs // 2 - 1,)),
            dma((slabs // 2 - 1,)),
            dma((slabs // 2 - 1,)),
            dma((slabs // 2 - 1,)),
        ],
        compiler_params=pltpu.CompilerParams(
            collective_id=0, has_side_effects=True, vmem_limit_bytes=48 << 20
        ),
        cost_estimate=pl.CostEstimate(flops=10 << 30, bytes_accessed=16 << 20, transcendentals=0),
        name="mix",
    )(mixed, weights, keys, gain, latents)


def per_device(
    tokens,
    refine_feat,
    refine_dest,
    refine_rows,
    conv_w,
    norm_gain,
    w_val,
    w_gate,
    latent_keys,
    latents,
):
    depth, side_y, side_x, width = tokens.shape
    row_count = depth * side_y * side_x
    slabs = lax.axis_size("slab")
    blocks, block_rows = refine_rows.shape
    capacity = max(2, (2 * blocks + slabs - 1) // slabs)
    slots = slabs * capacity

    up = [(i, i + 1) for i in range(slabs - 1)]
    down = [(i + 1, i) for i in range(slabs - 1)]
    before = lax.ppermute(tokens[-1:], "slab", up)
    after = lax.ppermute(tokens[:1], "slab", down)

    sent = pack(refine_dest[:, 0], refine_feat, refine_rows, slabs, capacity, row_count)
    received = lax.all_to_all(
        sent.reshape(slabs, capacity * (block_rows + EXTRA), width),
        "slab",
        split_axis=0,
        concat_axis=0,
        tiled=True,
    )
    received = received.reshape(slots, block_rows + EXTRA, width)

    base = conv(tokens, before, after, conv_w)
    weights = jnp.concatenate([w_val, w_gate], axis=1)

    mixed = scatter(base, received)
    assign, latent_new = mix(mixed, weights, latent_keys, norm_gain[None, :], latents)
    readback = jnp.dot(assign, latent_new.astype(BF16), preferred_element_type=F32)
    block_out = (mixed.astype(F32) + readback).astype(BF16)
    return (block_out.reshape(depth, side_y, side_x, width), latent_new)


def solution(mesh):
    return jax.shard_map(
        per_device,
        mesh=mesh,
        in_specs=(
            P("slab", None, None, "chan"),
            P("slab", None, "chan"),
            P("slab", None),
            P("slab", None),
            P(None, "chan"),
            P(),
            P(None, "chan"),
            P(None, "chan"),
            P(),
            P(None, "chan"),
        ),
        out_specs=(P("slab", None, None, "chan"), P(None, "chan")),
        check_vma=False,
    )
```

```python
import functools

import jax
import jax.numpy as jnp
from jax import lax
from jax.experimental import pallas as pl
from jax.experimental.pallas import tpu as pltpu
from jax.sharding import PartitionSpec as P


MESH = pl.DeviceIdType.MESH
BF16 = jnp.bfloat16
F32 = jnp.float32
EXTRA = 8


def whole():
    return pl.BlockSpec(memory_space=pltpu.VMEM)


def pack_kernel(
    capacity, empty, dest_ref, feat_ref, rows_ref, out_ref, taken, turn_of, feat, wide, codes, in_sems, out_sems, code_sem
):
    slabs, _, width = out_ref.shape
    blocks, rows, _ = feat_ref.shape
    pieces = in_sems.shape[0]
    each = blocks // pieces

    def fetch(i):
        part = pl.ds(i * each, each)
        return pltpu.make_async_copy(feat_ref.at[part], feat.at[part], in_sems.at[i])

    for i in range(pieces):
        fetch(i).start()

    def coded(number):
        both = jnp.concatenate([number // 128, number % 128], axis=1)
        return both.astype(F32)

    wide[...] = jnp.broadcast_to(coded(jnp.full((1, rows), empty, jnp.int32)), wide.shape)
    for t in range(slabs):
        taken[t] = 0

    def place(b, carry):
        to = dest_ref[b]
        turn = taken[to]
        taken[to] = turn + 1
        turn_of[b] = turn
        wide[pl.ds(to * EXTRA + turn, 1), :] = coded(rows_ref[pl.ds(b, 1), :])
        return carry

    lax.fori_loop(0, blocks, place, 0)
    codes[...] = wide[...].reshape(slabs, EXTRA, width).astype(BF16)
    code_copy = pltpu.make_async_copy(
        codes, out_ref.at[pl.ds(0, slabs), pl.ds(capacity * rows, EXTRA)], code_sem
    )
    code_copy.start()

    def put(b):
        return pltpu.make_async_copy(
            feat.at[b],
            out_ref.at[dest_ref[b], pl.ds(pl.multiple_of(turn_of[b] * rows, rows), rows)],
            out_sems.at[b],
        )

    def send(b, carry):
        put(b).start()
        return carry

    def finish(b, carry):
        put(b).wait()
        return carry

    for i in range(pieces):
        fetch(i).wait()
        lax.fori_loop(i * each, (i + 1) * each, send, 0)
    lax.fori_loop(0, blocks, finish, 0)
    code_copy.wait()


def pack(dest, feat, row_ids, slabs, capacity, empty):
    blocks, rows, width = feat.shape
    anywhere = pl.BlockSpec(memory_space=pl.ANY)
    dma = pltpu.SemaphoreType.DMA
    return pl.pallas_call(
        functools.partial(pack_kernel, capacity, empty),
        out_shape=jax.ShapeDtypeStruct((slabs, capacity * rows + EXTRA, width), BF16),
        in_specs=[pl.BlockSpec(memory_space=pltpu.SMEM), anywhere, whole()],
        out_specs=anywhere,
        scratch_shapes=[
            pltpu.SMEM((slabs,), jnp.int32),
            pltpu.SMEM((blocks,), jnp.int32),
            pltpu.VMEM(feat.shape, BF16),
            pltpu.VMEM((slabs * EXTRA, width), F32),
            pltpu.VMEM((slabs, EXTRA, width), BF16),
            dma((4,)),
            dma((blocks,)),
            dma,
        ],
        compiler_params=pltpu.CompilerParams(vmem_limit_bytes=60 << 20),
        cost_estimate=pl.CostEstimate(flops=0, bytes_accessed=6 << 20, transcendentals=0),
        name="pack",
    )(dest, feat, row_ids)


def conv_kernel(tokens_ref, before_ref, after_ref, w_ref, out_ref, plane):
    z = pl.program_id(0)
    last = pl.num_programs(0) - 1
    _, side_y, side_x, width = tokens_ref.shape

    def widen(slot, value):
        plane[slot, pl.ds(1, side_y)] = value.astype(F32)

    @pl.when(z == 0)
    def _():
        zero = jnp.zeros((side_x, width), F32)
        for slot in range(3):
            plane[slot, 0] = zero
            plane[slot, side_y + 1] = zero
        widen(2, before_ref[0])
        widen(0, tokens_ref[0])

    ahead = lax.rem(z + 1, 3)

    @pl.when(z < last)
    def _():
        widen(ahead, tokens_ref[z + 1])

    @pl.when(z == last)
    def _():
        widen(ahead, after_ref[0])

    slots = (lax.rem(z + 2, 3), lax.rem(z, 3), ahead)
    column = lax.broadcasted_iota(jnp.int32, (side_x, 128), 0)
    for half in range(width // 128):
        lanes = pl.ds(128 * half, 128)

        def one(y, carry):
            sums = [None, None, None]
            for dz in range(3):
                for dy in range(3):
                    row = plane[slots[dz], y + dy, :, lanes]
                    for dx in range(3):
                        k = 9 * dz + 3 * dy + dx
                        term = row * w_ref[pl.ds(k, 1), lanes]
                        sums[dx] = term if sums[dx] is None else sums[dx] + term
            centre = plane[slots[1], y + 1, :, lanes] + sums[1]
            left = jnp.where(column == 0, 0.0, pltpu.roll(sums[0], 1, 0))
            right = jnp.where(column == side_x - 1, 0.0, pltpu.roll(sums[2], side_x - 1, 0))
            value = centre + left + right
            for i in range(0, side_x, 8):
                to = pl.ds(pl.multiple_of(2 * side_x * y + 2 * i + 8 * half, 8), 8)
                out_ref[to, :] = value[i : i + 8]
            return carry

        lax.fori_loop(0, side_y, one, 0)


def conv(tokens, before, after, w):
    depth, side_y, side_x, width = tokens.shape
    rows = side_y * side_x
    fixed = lambda shape: pl.BlockSpec(shape, lambda z: (0,) * len(shape))
    return pl.pallas_call(
        conv_kernel,
        grid=(depth,),
        out_shape=jax.ShapeDtypeStruct((2 * depth * rows, 128), F32),
        in_specs=[fixed(tokens.shape), fixed(before.shape), fixed(after.shape), fixed(w.shape)],
        out_specs=pl.BlockSpec((2 * rows, 128), lambda z: (z, 0)),
        scratch_shapes=[pltpu.VMEM((3, side_y + 2, side_x, width), F32)],
        cost_estimate=pl.CostEstimate(
            flops=54 * depth * rows * width, bytes_accessed=30 << 20, transcendentals=0
        ),
        name="conv",
    )(tokens, before, after, w)


GROUP = 16


def scatter_kernel(
    base_ref,
    recv_ref,
    out_ref,
    acc,
    wide,
    feat,
    codes,
    spots,
    clash,
    out,
    spots_ref,
    clash_ref,
    feat_sems,
    base_sem,
    code_sems,
    out_sems,
):
    slots, block_rows, _ = feat.shape
    slabs = recv_ref.shape[0]
    capacity = slots // slabs
    total = acc.shape[0] // 2
    pieces = feat_sems.shape[0]
    each = slots // pieces
    step = 128

    code_copy = pltpu.make_async_copy(
        recv_ref.at[pl.ds(0, slabs), pl.ds(capacity * block_rows, EXTRA)], codes, code_sems.at[0]
    )
    code_copy.start()
    base_copy = pltpu.make_async_copy(base_ref, acc, base_sem)

    def fetch(i):
        return pltpu.make_async_copy(
            recv_ref.at[
                pl.ds(i * each % slabs, each),
                pl.ds(pl.multiple_of(i * each // slabs * block_rows, block_rows), block_rows),
            ],
            feat.at[pl.ds(i * each, each)],
            feat_sems.at[i],
        )

    base_copy.start()
    for i in range(pieces):
        fetch(i).start()

    code_copy.wait()
    coded = codes[...].astype(F32)
    turn = lax.broadcasted_iota(jnp.int32, coded.shape, 1)
    code = jnp.concatenate(
        [jnp.max(jnp.where(turn == k, coded, 0.0), axis=1) for k in range(capacity)], axis=0
    )
    number = (code[:, :block_rows] * 128.0 + code[:, block_rows:]).astype(jnp.int32)
    spots[...] = (number // 8) * 16 + number % 8
    lane = lax.broadcasted_iota(jnp.int32, number.shape, 1)
    again = jnp.zeros_like(number)
    for k in range(1, GROUP):
        same = (number == pltpu.roll(number, k, 1)) & (lane % GROUP >= k)
        again = jnp.where(same, 1, again)
    k = 1
    while k < GROUP:
        again = jnp.maximum(again, jnp.where(lane % GROUP >= k, pltpu.roll(again, k, 1), 0))
        k *= 2
    most = jnp.max(again.astype(F32), axis=1, keepdims=True).astype(jnp.int32)
    clash[...] = jnp.where(lane == 0, most, again)
    scalars = (
        pltpu.make_async_copy(spots, spots_ref, code_sems.at[1]),
        pltpu.make_async_copy(clash, clash_ref, code_sems.at[2]),
    )
    for copy in scalars:
        copy.start()
    for copy in scalars:
        copy.wait()
    base_copy.wait()

    def at(spot):
        return pl.ds(spot, 2, stride=8)

    def one(j, carry):
        @pl.when(lax.rem(j, each) == 0)
        def _():
            fetch(j // each).wait()

        @pl.when(spots_ref[j, 0] < 2 * total)
        def _():
            for k in range(0, block_rows, 16):
                for h in range(2):
                    value = feat[j, k : k + 16, 128 * h : 128 * h + 128].astype(F32)
                    wide[2 * k + 8 * h : 2 * k + 8 * h + 8, :] = value[:8]
                    wide[2 * k + 16 + 8 * h : 2 * k + 24 + 8 * h, :] = value[8:]

            groups = block_rows // GROUP
            mine = [2 * (c - c % 8) + c % 8 for c in range(block_rows)]

            def together(g):
                places = range(g * GROUP, (g + 1) * GROUP)
                where = [spots_ref[j, c] for c in places]
                news = [acc[at(r), :] + wide[at(mine[c]), :] for r, c in zip(where, places)]
                for r, new in zip(where, news):
                    acc[at(r), :] = new

            @pl.when(clash_ref[j, 0] == 0)
            def _():
                for g in range(groups):
                    together(g)

            @pl.when(clash_ref[j, 0] != 0)
            def _():
                for g in range(groups):

                    @pl.when(clash_ref[j, (g + 1) * GROUP - 1] == 0)
                    def _():
                        together(g)

                    @pl.when(clash_ref[j, (g + 1) * GROUP - 1] != 0)
                    def _():
                        for c in range(g * GROUP, (g + 1) * GROUP):
                            r = spots_ref[j, c]
                            acc[at(r), :] = acc[at(r), :] + wide[at(mine[c]), :]

        return carry

    lax.fori_loop(0, slots, one, 0)

    def finish(i, carry):
        value = acc[pl.ds(pl.multiple_of(i * 2 * step, 2 * step), 2 * step), :]
        value = value.reshape(step // 8, 2, 8, 128)
        part = pl.ds(pl.multiple_of(i * step, step), step)
        for h in range(2):
            out[part, 128 * h : 128 * h + 128] = value[:, h].reshape(step, 128).astype(BF16)
        return carry

    parts = out_sems.shape[0]
    share = total // parts

    def out_copy(p):
        rows = pl.ds(p * share, share)
        return pltpu.make_async_copy(out.at[rows], out_ref.at[rows], out_sems.at[p])

    for p in range(parts):
        lax.fori_loop(p * share // step, (p + 1) * share // step, finish, 0)
        out_copy(p).start()
    for p in range(parts):
        out_copy(p).wait()


def scatter(base, recv, capacity):
    total, width = base.shape[0] // 2, 2 * base.shape[1]
    slots, block_rows = capacity * recv.shape[0], (recv.shape[1] - EXTRA) // capacity
    anywhere = pl.BlockSpec(memory_space=pl.ANY)
    dma = pltpu.SemaphoreType.DMA
    return pl.pallas_call(
        scatter_kernel,
        out_shape=jax.ShapeDtypeStruct((total, width), BF16),
        in_specs=[anywhere, anywhere],
        out_specs=anywhere,
        scratch_shapes=[
            pltpu.VMEM((2 * total, 128), F32),
            pltpu.VMEM((2 * block_rows, 128), F32),
            pltpu.VMEM((slots, block_rows, width), BF16),
            pltpu.VMEM((recv.shape[0], EXTRA, width), BF16),
            pltpu.VMEM((slots, block_rows), jnp.int32),
            pltpu.VMEM((slots, block_rows), jnp.int32),
            pltpu.VMEM((total, width), BF16),
            pltpu.SMEM((slots, block_rows), jnp.int32),
            pltpu.SMEM((slots, block_rows), jnp.int32),
            dma((8,)),
            dma,
            dma((3,)),
            dma((4,)),
        ],
        compiler_params=pltpu.CompilerParams(vmem_limit_bytes=60 << 20),
        cost_estimate=pl.CostEstimate(flops=2 << 20, bytes_accessed=16 << 20, transcendentals=0),
        name="scatter",
    )(base, recv)


CHUNKS = 8


def mix_kernel(
    mixed_ref,
    w_ref,
    keys_ref,
    gain_ref,
    latents_ref,
    assign_ref,
    latent_ref,
    xbuf,
    nbuf,
    wbuf,
    own,
    pooled,
    totals,
    part_out,
    part_in,
    tile_out,
    tile_in,
    new_out,
    new_in,
    local_sem,
    x_send,
    x_recv,
    w_send,
    w_recv,
    a_send,
    a_recv,
    p_send,
    p_recv,
    t_send,
    t_recv,
    n_send,
    n_recv,
):
    slab = lax.axis_index("slab")
    chan = lax.axis_index("chan")
    slabs = lax.axis_size("slab")
    z_lo, core = chan // 2, chan % 2
    peers = (
        chan,
        z_lo * 2 + (1 - core),
        (1 - z_lo) * 2 + core,
        (1 - z_lo) * 2 + (1 - core),
    )
    far_slab = (slab + slabs // 2) % slabs
    quarter = xbuf.shape[1]
    size = quarter // CHUNKS
    width = xbuf.shape[2]
    half = slabs // 2
    z_hi, spot = slab // half, slab % half

    def local_copies():
        yield pltpu.make_async_copy(
            mixed_ref.at[pl.ds(chan * quarter, quarter)], xbuf.at[chan], local_sem.at[0]
        )
        yield pltpu.make_async_copy(w_ref, wbuf.at[chan], local_sem.at[1])

    for copy in local_copies():
        copy.start()

    barrier = pltpu.get_barrier_semaphore()
    for d in (1, 2, 3):
        for where in (slab, far_slab):
            pl.semaphore_signal(barrier, inc=1, device_id=(where, peers[d]), device_id_type=MESH)

    pl.semaphore_signal(barrier, inc=1, device_id=(far_slab, chan), device_id_type=MESH)

    def greet(k, carry):
        pl.semaphore_signal(
            barrier,
            inc=1,
            device_id=(z_hi * half + (spot + k) % half, chan),
            device_id_type=MESH,
        )
        return carry

    lax.fori_loop(1, half, greet, 0)
    pl.semaphore_wait(barrier, 7 + half - 1)

    def x_copy(d, i):
        rows = pl.ds(i * size, size)
        return pltpu.make_async_remote_copy(
            src_ref=mixed_ref.at[pl.ds(peers[d] * quarter + i * size, size)],
            dst_ref=xbuf.at[chan, rows],
            send_sem=x_send.at[d - 1, i],
            recv_sem=x_recv.at[d - 1, i],
            device_id=(slab, peers[d]),
            device_id_type=MESH,
        )

    def w_copy(which):
        source, device = (
            (w_ref, (slab, peers[1])),
            (w_ref, (far_slab, peers[2])),
            (wbuf.at[peers[2]], (slab, peers[1])),
        )[which]
        return pltpu.make_async_remote_copy(
            src_ref=source,
            dst_ref=wbuf.at[peers[2] if which == 2 else chan],
            send_sem=w_send.at[which],
            recv_sem=w_recv.at[which],
            device_id=device,
            device_id_type=MESH,
        )

    part_rows = quarter // 2

    def a_copy(d, i):
        return pltpu.make_async_remote_copy(
            src_ref=own.at[pl.ds(i * part_rows, part_rows)],
            dst_ref=assign_ref.at[pl.ds(chan * quarter + i * part_rows, part_rows)],
            send_sem=a_send.at[d - 1, i],
            recv_sem=a_recv.at[d - 1, i],
            device_id=(slab, peers[d]),
            device_id_type=MESH,
        )

    def start_x(i, carry):
        for d in (1, 2, 3):
            x_copy(d, i).start()
        return carry

    w_copy(1).start()
    lax.fori_loop(0, CHUNKS, start_x, 0)
    w_copy(0).start()
    pooled[...] = jnp.zeros_like(pooled)
    totals[...] = jnp.zeros_like(totals)
    for copy in local_copies():
        copy.wait()

    def assign_chunk(i):
        for d in (1, 2, 3):
            x_copy(d, i).wait_recv()
        rows = pl.ds(pl.multiple_of(i * size, size), size)
        wide = [xbuf[p, rows, :].astype(F32) for p in range(4)]
        square = sum(jnp.sum(v * v, axis=1, keepdims=True) for v in wide)
        scale = lax.rsqrt(square * (1.0 / (4 * width)) + 1e-06)
        for p in range(4):
            lanes = pl.ds(p * width, width)
            nbuf[rows, lanes] = (wide[p] * scale * gain_ref[:, lanes]).astype(BF16)
        scores = lax.dot_general(
            nbuf[rows, :], keys_ref[...], (((1,), (1,)), ((), ())), preferred_element_type=F32
        )
        scores = scores * (4 * width) ** (-0.5)
        top = jnp.max(scores, axis=1, keepdims=True)
        power = jnp.exp(scores - top)
        own[rows, :] = (power / jnp.sum(power, axis=1, keepdims=True)).astype(BF16)

    def pool_chunk(i):
        rows = pl.ds(pl.multiple_of(i * size, size), size)
        assign = own[rows, :]
        over_rows = (((0,), (0,)), ((), ()))
        totals[...] += jnp.dot(jnp.ones((16, size), BF16), assign, preferred_element_type=F32)
        for p in range(4):
            both = jnp.dot(nbuf[rows, :], wbuf[p], preferred_element_type=F32)
            gated = (both[:, :width] * jax.nn.sigmoid(both[:, width:])).astype(BF16)
            pooled[p] += lax.dot_general(assign, gated, over_rows, preferred_element_type=F32)

    def early(i, carry):
        assign_chunk(i)
        return carry

    lax.fori_loop(0, CHUNKS // 2, early, 0)
    w_copy(1).wait_recv()
    w_copy(2).start()
    w_copy(0).wait_recv()
    w_copy(2).wait_recv()

    def late(i, carry):
        assign_chunk(i + CHUNKS // 2)
        pool_chunk(2 * i)
        pool_chunk(2 * i + 1)
        return carry

    lax.fori_loop(0, CHUNKS // 2 - 1, late, 0)
    pool_chunk(CHUNKS - 2)
    assign_chunk(CHUNKS - 1)
    pool_chunk(CHUNKS - 1)

    column = [(far, d) for far in range(2) for d in range(4)][1:]
    held = pooled.shape[1]
    place = z_hi * 4 + chan

    def p_copy(n):
        far, d = column[n]
        return pltpu.make_async_remote_copy(
            src_ref=part_out.at[peers[d]],
            dst_ref=part_in.at[place],
            send_sem=p_send.at[n],
            recv_sem=p_recv.at[n],
            device_id=((slab + far * half) % slabs, peers[d]),
            device_id_type=MESH,
        )

    weights = totals[...].astype(BF16)
    for p in range(4):
        part_out[p, pl.ds(0, held)] = pooled[p].astype(BF16)
        part_out[p, pl.ds(held, 16), pl.ds(0, 128)] = weights
        part_out[p, pl.ds(held, 16), pl.ds(128, width - 128)] = jnp.zeros((16, width - 128), BF16)
    for n in (4, 1, 2, 5, 6, 3, 0):
        p_copy(n).start()
    for i in range(2):
        for d in (2, 1):
            a_copy(d, i).start()
    keep = pltpu.make_async_copy(own, assign_ref.at[pl.ds(chan * quarter, quarter)], local_sem.at[0])
    keep.start()
    part_in[place] = part_out[chan]
    for n in range(7):
        p_copy(n).wait_recv()
    mine = part_in[0, pl.ds(0, held)].astype(F32)
    total = part_in[0, pl.ds(held, 16), pl.ds(0, 128)].astype(F32)
    for n in range(1, 8):
        mine = mine + part_in[n, pl.ds(0, held)].astype(F32)
        total = total + part_in[n, pl.ds(held, 16), pl.ds(0, 128)].astype(F32)

    for t in range(half):
        for h in range(2):
            tile_out[t, h] = mine[8 * t : 8 * t + 8, 128 * h : 128 * h + 128]
        tile_out[t, 2] = total[:8]

    def plane_copy(k, source, target, send, recv):
        return pltpu.make_async_remote_copy(
            src_ref=source,
            dst_ref=target.at[spot],
            send_sem=send.at[k - 1],
            recv_sem=recv.at[k - 1],
            device_id=(z_hi * half + (spot + k) % half, chan),
            device_id_type=MESH,
        )

    def t_copy(k):
        return plane_copy(k, tile_out.at[(spot + k) % half], tile_in, t_send, t_recv)

    def n_copy(k):
        return plane_copy(k, new_out, new_in, n_send, n_recv)

    def over(number, action):
        def body(k, carry):
            action(k)
            return carry

        lax.fori_loop(1, number, body, 0)

    over(half, lambda k: t_copy(k).start())
    tile_in[spot] = tile_out[spot]
    over(half, lambda k: t_copy(k).wait_recv())
    sums = jnp.sum(tile_in[...], axis=0)
    first = 8 * spot
    row = lax.broadcasted_iota(jnp.int32, (8, 128), 0)
    lane = lax.broadcasted_iota(jnp.int32, (8, 128), 1)
    weight = jnp.sum(jnp.where(lane == row + first, sums[2], 0.0), axis=1, keepdims=True)
    for h in range(2):
        before = latents_ref[
            pl.ds(pl.multiple_of(first, 8), 8), pl.ds(128 * h, 128)
        ]
        new_out[h] = before + sums[h] / (weight + 1.0)
    over(half, lambda k: n_copy(k).start())
    new_in[spot] = new_out[...]

    def forward(i):
        rows = pl.ds(peers[2] * quarter + i * part_rows, part_rows)
        return pltpu.make_async_remote_copy(
            src_ref=assign_ref.at[rows],
            dst_ref=assign_ref.at[rows],
            send_sem=a_send.at[2, i],
            recv_sem=a_recv.at[2, i],
            device_id=(slab, peers[1]),
            device_id_type=MESH,
        )

    for i in range(2):
        a_copy(2, i).wait_recv()
        forward(i).start()

    over(half, lambda k: n_copy(k).wait_recv())
    for t in range(half):
        for h in range(2):
            latent_ref[8 * t : 8 * t + 8, 128 * h : 128 * h + 128] = new_in[t, h]

    def drained(i, carry):
        for d in (1, 2, 3):
            x_copy(d, i).wait_send()
        return carry

    lax.fori_loop(0, CHUNKS, drained, 0)
    for which in range(3):
        w_copy(which).wait_send()
    for n in range(7):
        p_copy(n).wait_send()
    over(half, lambda k: t_copy(k).wait_send())
    over(half, lambda k: n_copy(k).wait_send())
    for i in range(2):
        a_copy(1, i).wait_recv()
        for d in (1, 2):
            a_copy(d, i).wait_send()
        forward(i).wait()
    keep.wait()


def mix(mixed, weights, keys, gain, latents):
    rows, width = mixed.shape
    slabs = lax.axis_size("slab")
    quarter = rows // 4
    held = latents.shape[0]
    dma = pltpu.SemaphoreType.DMA
    return pl.pallas_call(
        mix_kernel,
        out_shape=(
            jax.ShapeDtypeStruct((rows, held), BF16),
            jax.ShapeDtypeStruct((held, width), F32),
        ),
        in_specs=[
            pl.BlockSpec(memory_space=pl.ANY),
            pl.BlockSpec(memory_space=pl.ANY),
            whole(),
            whole(),
            whole(),
        ],
        out_specs=(pl.BlockSpec(memory_space=pl.ANY), whole()),
        scratch_shapes=[
            pltpu.VMEM((4, quarter, width), BF16),
            pltpu.VMEM((quarter, 4 * width), BF16),
            pltpu.VMEM((4,) + weights.shape, BF16),
            pltpu.VMEM((quarter, held), BF16),
            pltpu.VMEM((4, held, width), F32),
            pltpu.VMEM((16, 128), F32),
            pltpu.VMEM((4, held + 16, width), BF16),
            pltpu.VMEM((8, held + 16, width), BF16),
            pltpu.VMEM((slabs // 2, 3, 8, 128), F32),
            pltpu.VMEM((slabs // 2, 3, 8, 128), F32),
            pltpu.VMEM((2, 8, 128), F32),
            pltpu.VMEM((slabs // 2, 2, 8, 128), F32),
            dma((2,)),
            dma((3, CHUNKS)),
            dma((3, CHUNKS)),
            dma((3,)),
            dma((3,)),
            dma((3, 2)),
            dma((3, 2)),
            dma((7,)),
            dma((7,)),
            dma((slabs // 2 - 1,)),
            dma((slabs // 2 - 1,)),
            dma((slabs // 2 - 1,)),
            dma((slabs // 2 - 1,)),
        ],
        compiler_params=pltpu.CompilerParams(
            collective_id=0, has_side_effects=True, vmem_limit_bytes=48 << 20
        ),
        cost_estimate=pl.CostEstimate(flops=10 << 30, bytes_accessed=16 << 20, transcendentals=0),
        name="mix",
    )(mixed, weights, keys, gain, latents)


def per_device(
    tokens,
    refine_feat,
    refine_dest,
    refine_rows,
    conv_w,
    norm_gain,
    w_val,
    w_gate,
    latent_keys,
    latents,
):
    depth, side_y, side_x, width = tokens.shape
    row_count = depth * side_y * side_x
    slabs = lax.axis_size("slab")
    blocks, _ = refine_rows.shape
    capacity = max(2, (2 * blocks + slabs - 1) // slabs)

    up = [(i, i + 1) for i in range(slabs - 1)]
    down = [(i + 1, i) for i in range(slabs - 1)]
    before = lax.ppermute(tokens[-1:], "slab", up)
    after = lax.ppermute(tokens[:1], "slab", down)

    sent = pack(refine_dest[:, 0], refine_feat, refine_rows, slabs, capacity, row_count)
    received = lax.all_to_all(
        sent,
        "slab",
        split_axis=0,
        concat_axis=0,
        tiled=True,
    )

    base = conv(tokens, before, after, conv_w)
    weights = jnp.concatenate([w_val, w_gate], axis=1)

    mixed = scatter(base, received, capacity)
    assign, latent_new = mix(mixed, weights, latent_keys, norm_gain[None, :], latents)
    readback = jnp.dot(assign, latent_new.astype(BF16), preferred_element_type=F32)
    block_out = (mixed.astype(F32) + readback).astype(BF16)
    return (block_out.reshape(depth, side_y, side_x, width), latent_new)


def solution(mesh):
    return jax.shard_map(
        per_device,
        mesh=mesh,
        in_specs=(
            P("slab", None, None, "chan"),
            P("slab", None, "chan"),
            P("slab", None),
            P("slab", None),
            P(None, "chan"),
            P(),
            P(None, "chan"),
            P(None, "chan"),
            P(),
            P(None, "chan"),
        ),
        out_specs=(P("slab", None, None, "chan"), P(None, "chan")),
        check_vma=False,
    )
```

```python
import functools

import jax
import jax.numpy as jnp
from jax import lax
from jax.experimental import pallas as pl
from jax.experimental.pallas import tpu as pltpu
from jax.sharding import PartitionSpec as P


MESH = pl.DeviceIdType.MESH
BF16 = jnp.bfloat16
F32 = jnp.float32
EXTRA = 8


def whole():
    return pl.BlockSpec(memory_space=pltpu.VMEM)


def pack_kernel(
    capacity, empty, dest_ref, feat_ref, rows_ref, out_ref, taken, turn_of, feat, wide, codes, in_sems, out_sems, code_sem
):
    slabs, _, width = out_ref.shape
    blocks, rows, _ = feat_ref.shape
    pieces = in_sems.shape[0]
    each = blocks // pieces

    def fetch(i):
        part = pl.ds(i * each, each)
        return pltpu.make_async_copy(feat_ref.at[part], feat.at[part], in_sems.at[i])

    for i in range(pieces):
        fetch(i).start()

    def coded(number):
        both = jnp.concatenate([number // 128, number % 128], axis=1)
        return both.astype(F32)

    wide[...] = jnp.broadcast_to(coded(jnp.full((1, rows), empty, jnp.int32)), wide.shape)
    for t in range(slabs):
        taken[t] = 0

    def place(b, carry):
        to = dest_ref[b]
        turn = taken[to]
        taken[to] = turn + 1
        turn_of[b] = turn
        wide[pl.ds(to * EXTRA + turn, 1), :] = coded(rows_ref[pl.ds(b, 1), :])
        return carry

    lax.fori_loop(0, blocks, place, 0)
    codes[...] = wide[...].reshape(slabs, EXTRA, width).astype(BF16)
    code_copy = pltpu.make_async_copy(
        codes, out_ref.at[pl.ds(0, slabs), pl.ds(capacity * rows, EXTRA)], code_sem
    )
    code_copy.start()

    def put(b):
        return pltpu.make_async_copy(
            feat.at[b],
            out_ref.at[dest_ref[b], pl.ds(pl.multiple_of(turn_of[b] * rows, rows), rows)],
            out_sems.at[b],
        )

    def send(b, carry):
        put(b).start()
        return carry

    def finish(b, carry):
        put(b).wait()
        return carry

    for i in range(pieces):
        fetch(i).wait()
        lax.fori_loop(i * each, (i + 1) * each, send, 0)
    lax.fori_loop(0, blocks, finish, 0)
    code_copy.wait()


def pack(dest, feat, row_ids, slabs, capacity, empty):
    blocks, rows, width = feat.shape
    anywhere = pl.BlockSpec(memory_space=pl.ANY)
    dma = pltpu.SemaphoreType.DMA
    return pl.pallas_call(
        functools.partial(pack_kernel, capacity, empty),
        out_shape=jax.ShapeDtypeStruct((slabs, capacity * rows + EXTRA, width), BF16),
        in_specs=[pl.BlockSpec(memory_space=pltpu.SMEM), anywhere, whole()],
        out_specs=anywhere,
        scratch_shapes=[
            pltpu.SMEM((slabs,), jnp.int32),
            pltpu.SMEM((blocks,), jnp.int32),
            pltpu.VMEM(feat.shape, BF16),
            pltpu.VMEM((slabs * EXTRA, width), F32),
            pltpu.VMEM((slabs, EXTRA, width), BF16),
            dma((4,)),
            dma((blocks,)),
            dma,
        ],
        compiler_params=pltpu.CompilerParams(vmem_limit_bytes=60 << 20),
        cost_estimate=pl.CostEstimate(flops=0, bytes_accessed=6 << 20, transcendentals=0),
        name="pack",
    )(dest, feat, row_ids)


def conv_kernel(tokens_ref, before_ref, after_ref, w_ref, out_ref, plane):
    z = pl.program_id(0)
    last = pl.num_programs(0) - 1
    _, side_y, side_x, width = tokens_ref.shape

    def widen(slot, value):
        plane[slot, pl.ds(1, side_y)] = value.astype(F32)

    @pl.when(z == 0)
    def _():
        zero = jnp.zeros((side_x, width), F32)
        for slot in range(3):
            plane[slot, 0] = zero
            plane[slot, side_y + 1] = zero
        widen(2, before_ref[0])
        widen(0, tokens_ref[0])

    ahead = lax.rem(z + 1, 3)

    @pl.when(z < last)
    def _():
        widen(ahead, tokens_ref[z + 1])

    @pl.when(z == last)
    def _():
        widen(ahead, after_ref[0])

    slots = (lax.rem(z + 2, 3), lax.rem(z, 3), ahead)
    column = lax.broadcasted_iota(jnp.int32, (side_x, 128), 0)
    for half in range(width // 128):
        lanes = pl.ds(128 * half, 128)

        def one(y, carry):
            sums = [None, None, None]
            for dz in range(3):
                for dy in range(3):
                    row = plane[slots[dz], y + dy, :, lanes]
                    for dx in range(3):
                        k = 9 * dz + 3 * dy + dx
                        term = row * w_ref[pl.ds(k, 1), lanes]
                        sums[dx] = term if sums[dx] is None else sums[dx] + term
            centre = plane[slots[1], y + 1, :, lanes] + sums[1]
            left = jnp.where(column == 0, 0.0, pltpu.roll(sums[0], 1, 0))
            right = jnp.where(column == side_x - 1, 0.0, pltpu.roll(sums[2], side_x - 1, 0))
            value = centre + left + right
            for i in range(0, side_x, 8):
                to = pl.ds(pl.multiple_of(2 * side_x * y + 2 * i + 8 * half, 8), 8)
                out_ref[to, :] = value[i : i + 8]
            return carry

        lax.fori_loop(0, side_y, one, 0)


def conv(tokens, before, after, w):
    depth, side_y, side_x, width = tokens.shape
    rows = side_y * side_x
    fixed = lambda shape: pl.BlockSpec(shape, lambda z: (0,) * len(shape))
    return pl.pallas_call(
        conv_kernel,
        grid=(depth,),
        out_shape=jax.ShapeDtypeStruct((2 * depth * rows, 128), F32),
        in_specs=[fixed(tokens.shape), fixed(before.shape), fixed(after.shape), fixed(w.shape)],
        out_specs=pl.BlockSpec((2 * rows, 128), lambda z: (z, 0)),
        scratch_shapes=[pltpu.VMEM((3, side_y + 2, side_x, width), F32)],
        cost_estimate=pl.CostEstimate(
            flops=54 * depth * rows * width, bytes_accessed=30 << 20, transcendentals=0
        ),
        name="conv",
    )(tokens, before, after, w)


GROUP = 16


def scatter_kernel(
    base_ref,
    recv_ref,
    out_ref,
    acc,
    wide,
    feat,
    codes,
    spots,
    clash,
    out,
    spots_ref,
    clash_ref,
    feat_sems,
    base_sem,
    code_sems,
    out_sems,
):
    slots, block_rows, _ = feat.shape
    slabs = recv_ref.shape[0]
    capacity = slots // slabs
    total = acc.shape[0] // 2
    pieces = feat_sems.shape[0]
    each = slots // pieces
    step = 128

    code_copy = pltpu.make_async_copy(
        recv_ref.at[pl.ds(0, slabs), pl.ds(capacity * block_rows, EXTRA)], codes, code_sems.at[0]
    )
    code_copy.start()
    base_copy = pltpu.make_async_copy(base_ref, acc, base_sem)

    def fetch(i):
        return pltpu.make_async_copy(
            recv_ref.at[
                pl.ds(i * each % slabs, each),
                pl.ds(pl.multiple_of(i * each // slabs * block_rows, block_rows), block_rows),
            ],
            feat.at[pl.ds(i * each, each)],
            feat_sems.at[i],
        )

    base_copy.start()
    for i in range(pieces):
        fetch(i).start()

    code_copy.wait()
    coded = codes[...].astype(F32)
    turn = lax.broadcasted_iota(jnp.int32, coded.shape, 1)
    code = jnp.concatenate(
        [jnp.max(jnp.where(turn == k, coded, 0.0), axis=1) for k in range(capacity)], axis=0
    )
    number = (code[:, :block_rows] * 128.0 + code[:, block_rows:]).astype(jnp.int32)
    spots[...] = (number // 8) * 16 + number % 8
    lane = lax.broadcasted_iota(jnp.int32, number.shape, 1)
    again = jnp.zeros_like(number)
    for k in range(1, GROUP):
        same = (number == pltpu.roll(number, k, 1)) & (lane % GROUP >= k)
        again = jnp.where(same, 1, again)
    k = 1
    while k < GROUP:
        again = jnp.maximum(again, jnp.where(lane % GROUP >= k, pltpu.roll(again, k, 1), 0))
        k *= 2
    most = jnp.max(again.astype(F32), axis=1, keepdims=True).astype(jnp.int32)
    clash[...] = jnp.where(lane == 0, most, again)
    scalars = (
        pltpu.make_async_copy(spots, spots_ref, code_sems.at[1]),
        pltpu.make_async_copy(clash, clash_ref, code_sems.at[2]),
    )
    for copy in scalars:
        copy.start()
    for copy in scalars:
        copy.wait()
    base_copy.wait()

    def at(spot):
        return pl.ds(spot, 2, stride=8)

    def one(j, carry):
        @pl.when(lax.rem(j, each) == 0)
        def _():
            fetch(j // each).wait()

        @pl.when(spots_ref[j, 0] < 2 * total)
        def _():
            for k in range(0, block_rows, 16):
                for h in range(2):
                    value = feat[j, k : k + 16, 128 * h : 128 * h + 128].astype(F32)
                    wide[2 * k + 8 * h : 2 * k + 8 * h + 8, :] = value[:8]
                    wide[2 * k + 16 + 8 * h : 2 * k + 24 + 8 * h, :] = value[8:]

            groups = block_rows // GROUP
            mine = [2 * (c - c % 8) + c % 8 for c in range(block_rows)]

            def together(g):
                places = range(g * GROUP, (g + 1) * GROUP)
                where = [spots_ref[j, c] for c in places]
                news = [acc[at(r), :] + wide[at(mine[c]), :] for r, c in zip(where, places)]
                for r, new in zip(where, news):
                    acc[at(r), :] = new

            @pl.when(clash_ref[j, 0] == 0)
            def _():
                for g in range(groups):
                    together(g)

            @pl.when(clash_ref[j, 0] != 0)
            def _():
                for g in range(groups):

                    @pl.when(clash_ref[j, (g + 1) * GROUP - 1] == 0)
                    def _():
                        together(g)

                    @pl.when(clash_ref[j, (g + 1) * GROUP - 1] != 0)
                    def _():
                        for c in range(g * GROUP, (g + 1) * GROUP):
                            r = spots_ref[j, c]
                            acc[at(r), :] = acc[at(r), :] + wide[at(mine[c]), :]

        return carry

    lax.fori_loop(0, slots, one, 0)

    def finish(i, carry):
        value = acc[pl.ds(pl.multiple_of(i * 2 * step, 2 * step), 2 * step), :]
        value = value.reshape(step // 8, 2, 8, 128)
        part = pl.ds(pl.multiple_of(i * step, step), step)
        for h in range(2):
            out[part, 128 * h : 128 * h + 128] = value[:, h].reshape(step, 128).astype(BF16)
        return carry

    parts = out_sems.shape[0]
    share = total // parts

    def out_copy(p):
        rows = pl.ds(p * share, share)
        return pltpu.make_async_copy(out.at[rows], out_ref.at[rows], out_sems.at[p])

    for p in range(parts):
        lax.fori_loop(p * share // step, (p + 1) * share // step, finish, 0)
        out_copy(p).start()
    for p in range(parts):
        out_copy(p).wait()


def scatter(base, recv, capacity):
    total, width = base.shape[0] // 2, 2 * base.shape[1]
    slots, block_rows = capacity * recv.shape[0], (recv.shape[1] - EXTRA) // capacity
    anywhere = pl.BlockSpec(memory_space=pl.ANY)
    dma = pltpu.SemaphoreType.DMA
    return pl.pallas_call(
        scatter_kernel,
        out_shape=jax.ShapeDtypeStruct((total, width), BF16),
        in_specs=[anywhere, anywhere],
        out_specs=anywhere,
        scratch_shapes=[
            pltpu.VMEM((2 * total, 128), F32),
            pltpu.VMEM((2 * block_rows, 128), F32),
            pltpu.VMEM((slots, block_rows, width), BF16),
            pltpu.VMEM((recv.shape[0], EXTRA, width), BF16),
            pltpu.VMEM((slots, block_rows), jnp.int32),
            pltpu.VMEM((slots, block_rows), jnp.int32),
            pltpu.VMEM((total, width), BF16),
            pltpu.SMEM((slots, block_rows), jnp.int32),
            pltpu.SMEM((slots, block_rows), jnp.int32),
            dma((8,)),
            dma,
            dma((3,)),
            dma((4,)),
        ],
        compiler_params=pltpu.CompilerParams(vmem_limit_bytes=60 << 20),
        cost_estimate=pl.CostEstimate(flops=2 << 20, bytes_accessed=16 << 20, transcendentals=0),
        name="scatter",
    )(base, recv)


CHUNKS = 8


def mix_kernel(
    mixed_ref,
    w_ref,
    keys_ref,
    gain_ref,
    latents_ref,
    assign_ref,
    latent_ref,
    xbuf,
    nbuf,
    wbuf,
    own,
    pooled,
    totals,
    part_out,
    part_in,
    tile_out,
    tile_in,
    new_out,
    new_in,
    local_sem,
    x_send,
    x_recv,
    w_send,
    w_recv,
    a_send,
    a_recv,
    p_send,
    p_recv,
    t_send,
    t_recv,
    n_send,
    n_recv,
):
    slab = lax.axis_index("slab")
    chan = lax.axis_index("chan")
    slabs = lax.axis_size("slab")
    z_lo, core = chan // 2, chan % 2
    peers = (
        chan,
        z_lo * 2 + (1 - core),
        (1 - z_lo) * 2 + core,
        (1 - z_lo) * 2 + (1 - core),
    )
    far_slab = (slab + slabs // 2) % slabs
    quarter = xbuf.shape[1]
    size = quarter // CHUNKS
    width = xbuf.shape[2]
    half = slabs // 2
    z_hi, spot = slab // half, slab % half

    def local_copies():
        yield pltpu.make_async_copy(
            mixed_ref.at[pl.ds(chan * quarter, quarter)], xbuf.at[chan], local_sem.at[0]
        )
        yield pltpu.make_async_copy(w_ref, wbuf.at[chan], local_sem.at[1])

    for copy in local_copies():
        copy.start()

    barrier = pltpu.get_barrier_semaphore()
    for d in (1, 2, 3):
        for where in (slab, far_slab):
            pl.semaphore_signal(barrier, inc=1, device_id=(where, peers[d]), device_id_type=MESH)

    pl.semaphore_signal(barrier, inc=1, device_id=(far_slab, chan), device_id_type=MESH)

    def greet(k, carry):
        pl.semaphore_signal(
            barrier,
            inc=1,
            device_id=(z_hi * half + (spot + k) % half, chan),
            device_id_type=MESH,
        )
        return carry

    lax.fori_loop(1, half, greet, 0)
    pl.semaphore_wait(barrier, 7 + half - 1)

    def x_copy(d, i):
        rows = pl.ds(i * size, size)
        return pltpu.make_async_remote_copy(
            src_ref=mixed_ref.at[pl.ds(peers[d] * quarter + i * size, size)],
            dst_ref=xbuf.at[chan, rows],
            send_sem=x_send.at[d - 1, i],
            recv_sem=x_recv.at[d - 1, i],
            device_id=(slab, peers[d]),
            device_id_type=MESH,
        )

    def w_copy(which):
        source, device = (
            (w_ref, (slab, peers[1])),
            (w_ref, (far_slab, peers[2])),
            (wbuf.at[peers[2]], (slab, peers[1])),
        )[which]
        return pltpu.make_async_remote_copy(
            src_ref=source,
            dst_ref=wbuf.at[peers[2] if which == 2 else chan],
            send_sem=w_send.at[which],
            recv_sem=w_recv.at[which],
            device_id=device,
            device_id_type=MESH,
        )

    part_rows = quarter // 2

    def a_copy(d, i):
        return pltpu.make_async_remote_copy(
            src_ref=own.at[pl.ds(i * part_rows, part_rows)],
            dst_ref=assign_ref.at[pl.ds(chan * quarter + i * part_rows, part_rows)],
            send_sem=a_send.at[d - 1, i],
            recv_sem=a_recv.at[d - 1, i],
            device_id=(slab, peers[d]),
            device_id_type=MESH,
        )

    def start_x(i, carry):
        for d in (1, 2, 3):
            x_copy(d, i).start()
        return carry

    w_copy(1).start()
    lax.fori_loop(0, CHUNKS, start_x, 0)
    w_copy(0).start()
    pooled[...] = jnp.zeros_like(pooled)
    totals[...] = jnp.zeros_like(totals)
    for copy in local_copies():
        copy.wait()

    def assign_chunk(i):
        for d in (1, 2, 3):
            x_copy(d, i).wait_recv()
        rows = pl.ds(pl.multiple_of(i * size, size), size)
        wide = [xbuf[p, rows, :].astype(F32) for p in range(4)]
        square = sum(jnp.sum(v * v, axis=1, keepdims=True) for v in wide)
        scale = lax.rsqrt(square * (1.0 / (4 * width)) + 1e-06)
        for p in range(4):
            lanes = pl.ds(p * width, width)
            nbuf[rows, lanes] = (wide[p] * scale * gain_ref[:, lanes]).astype(BF16)
        scores = lax.dot_general(
            nbuf[rows, :], keys_ref[...], (((1,), (1,)), ((), ())), preferred_element_type=F32
        )
        scores = scores * (4 * width) ** (-0.5)
        top = jnp.max(scores, axis=1, keepdims=True)
        power = jnp.exp(scores - top)
        own[rows, :] = (power / jnp.sum(power, axis=1, keepdims=True)).astype(BF16)

    def pool_chunk(i):
        rows = pl.ds(pl.multiple_of(i * size, size), size)
        assign = own[rows, :]
        over_rows = (((0,), (0,)), ((), ()))
        totals[...] += jnp.dot(jnp.ones((16, size), BF16), assign, preferred_element_type=F32)
        for p in range(4):
            both = jnp.dot(nbuf[rows, :], wbuf[p], preferred_element_type=F32)
            gated = (both[:, :width] * jax.nn.sigmoid(both[:, width:])).astype(BF16)
            pooled[p] += lax.dot_general(assign, gated, over_rows, preferred_element_type=F32)

    def early(i, carry):
        assign_chunk(i)
        return carry

    lax.fori_loop(0, CHUNKS // 2, early, 0)
    a_copy(1, 0).start()
    w_copy(1).wait_recv()
    w_copy(2).start()
    w_copy(0).wait_recv()
    w_copy(2).wait_recv()

    def late(i, carry):
        assign_chunk(i + CHUNKS // 2)
        pool_chunk(2 * i)
        pool_chunk(2 * i + 1)
        return carry

    lax.fori_loop(0, CHUNKS // 2 - 1, late, 0)
    pool_chunk(CHUNKS - 2)
    assign_chunk(CHUNKS - 1)
    pool_chunk(CHUNKS - 1)

    column = [(far, d) for far in range(2) for d in range(4)][1:]
    held = pooled.shape[1]
    place = z_hi * 4 + chan

    def p_copy(n):
        far, d = column[n]
        return pltpu.make_async_remote_copy(
            src_ref=part_out.at[peers[d]],
            dst_ref=part_in.at[place],
            send_sem=p_send.at[n],
            recv_sem=p_recv.at[n],
            device_id=((slab + far * half) % slabs, peers[d]),
            device_id_type=MESH,
        )

    weights = totals[...].astype(BF16)
    for p in range(4):
        part_out[p, pl.ds(0, held)] = pooled[p].astype(BF16)
        part_out[p, pl.ds(held, 16), pl.ds(0, 128)] = weights
        part_out[p, pl.ds(held, 16), pl.ds(128, width - 128)] = jnp.zeros((16, width - 128), BF16)
    for n in (4, 1, 2, 5, 6, 3, 0):
        p_copy(n).start()
    for i in range(2):
        a_copy(2, i).start()
    a_copy(1, 1).start()
    keep = pltpu.make_async_copy(own, assign_ref.at[pl.ds(chan * quarter, quarter)], local_sem.at[0])
    keep.start()
    part_in[place] = part_out[chan]
    for n in range(7):
        p_copy(n).wait_recv()
    mine = part_in[0, pl.ds(0, held)].astype(F32)
    total = part_in[0, pl.ds(held, 16), pl.ds(0, 128)].astype(F32)
    for n in range(1, 8):
        mine = mine + part_in[n, pl.ds(0, held)].astype(F32)
        total = total + part_in[n, pl.ds(held, 16), pl.ds(0, 128)].astype(F32)

    for t in range(half):
        for h in range(2):
            tile_out[t, h] = mine[8 * t : 8 * t + 8, 128 * h : 128 * h + 128]
        tile_out[t, 2] = total[:8]

    def plane_copy(k, source, target, send, recv):
        return pltpu.make_async_remote_copy(
            src_ref=source,
            dst_ref=target.at[spot],
            send_sem=send.at[k - 1],
            recv_sem=recv.at[k - 1],
            device_id=(z_hi * half + (spot + k) % half, chan),
            device_id_type=MESH,
        )

    def t_copy(k):
        return plane_copy(k, tile_out.at[(spot + k) % half], tile_in, t_send, t_recv)

    def n_copy(k):
        return plane_copy(k, new_out, new_in, n_send, n_recv)

    def over(number, action):
        def body(k, carry):
            action(k)
            return carry

        lax.fori_loop(1, number, body, 0)

    over(half, lambda k: t_copy(k).start())
    tile_in[spot] = tile_out[spot]
    over(half, lambda k: t_copy(k).wait_recv())
    sums = jnp.sum(tile_in[...], axis=0)
    first = 8 * spot
    row = lax.broadcasted_iota(jnp.int32, (8, 128), 0)
    lane = lax.broadcasted_iota(jnp.int32, (8, 128), 1)
    weight = jnp.sum(jnp.where(lane == row + first, sums[2], 0.0), axis=1, keepdims=True)
    for h in range(2):
        before = latents_ref[
            pl.ds(pl.multiple_of(first, 8), 8), pl.ds(128 * h, 128)
        ]
        new_out[h] = before + sums[h] / (weight + 1.0)
    over(half, lambda k: n_copy(k).start())
    new_in[spot] = new_out[...]

    def forward(i):
        rows = pl.ds(peers[2] * quarter + i * part_rows, part_rows)
        return pltpu.make_async_remote_copy(
            src_ref=assign_ref.at[rows],
            dst_ref=assign_ref.at[rows],
            send_sem=a_send.at[2, i],
            recv_sem=a_recv.at[2, i],
            device_id=(slab, peers[1]),
            device_id_type=MESH,
        )

    for i in range(2):
        a_copy(2, i).wait_recv()
        forward(i).start()

    over(half, lambda k: n_copy(k).wait_recv())
    for t in range(half):
        for h in range(2):
            latent_ref[8 * t : 8 * t + 8, 128 * h : 128 * h + 128] = new_in[t, h]

    def drained(i, carry):
        for d in (1, 2, 3):
            x_copy(d, i).wait_send()
        return carry

    lax.fori_loop(0, CHUNKS, drained, 0)
    for which in range(3):
        w_copy(which).wait_send()
    for n in range(7):
        p_copy(n).wait_send()
    over(half, lambda k: t_copy(k).wait_send())
    over(half, lambda k: n_copy(k).wait_send())
    for i in range(2):
        a_copy(1, i).wait_recv()
        for d in (1, 2):
            a_copy(d, i).wait_send()
        forward(i).wait()
    keep.wait()


def mix(mixed, weights, keys, gain, latents):
    rows, width = mixed.shape
    slabs = lax.axis_size("slab")
    quarter = rows // 4
    held = latents.shape[0]
    dma = pltpu.SemaphoreType.DMA
    return pl.pallas_call(
        mix_kernel,
        out_shape=(
            jax.ShapeDtypeStruct((rows, held), BF16),
            jax.ShapeDtypeStruct((held, width), F32),
        ),
        in_specs=[
            pl.BlockSpec(memory_space=pl.ANY),
            pl.BlockSpec(memory_space=pl.ANY),
            whole(),
            whole(),
            whole(),
        ],
        out_specs=(pl.BlockSpec(memory_space=pl.ANY), whole()),
        scratch_shapes=[
            pltpu.VMEM((4, quarter, width), BF16),
            pltpu.VMEM((quarter, 4 * width), BF16),
            pltpu.VMEM((4,) + weights.shape, BF16),
            pltpu.VMEM((quarter, held), BF16),
            pltpu.VMEM((4, held, width), F32),
            pltpu.VMEM((16, 128), F32),
            pltpu.VMEM((4, held + 16, width), BF16),
            pltpu.VMEM((8, held + 16, width), BF16),
            pltpu.VMEM((slabs // 2, 3, 8, 128), F32),
            pltpu.VMEM((slabs // 2, 3, 8, 128), F32),
            pltpu.VMEM((2, 8, 128), F32),
            pltpu.VMEM((slabs // 2, 2, 8, 128), F32),
            dma((2,)),
            dma((3, CHUNKS)),
            dma((3, CHUNKS)),
            dma((3,)),
            dma((3,)),
            dma((3, 2)),
            dma((3, 2)),
            dma((7,)),
            dma((7,)),
            dma((slabs // 2 - 1,)),
            dma((slabs // 2 - 1,)),
            dma((slabs // 2 - 1,)),
            dma((slabs // 2 - 1,)),
        ],
        compiler_params=pltpu.CompilerParams(
            collective_id=0, has_side_effects=True, vmem_limit_bytes=48 << 20
        ),
        cost_estimate=pl.CostEstimate(flops=10 << 30, bytes_accessed=16 << 20, transcendentals=0),
        name="mix",
    )(mixed, weights, keys, gain, latents)


def per_device(
    tokens,
    refine_feat,
    refine_dest,
    refine_rows,
    conv_w,
    norm_gain,
    w_val,
    w_gate,
    latent_keys,
    latents,
):
    depth, side_y, side_x, width = tokens.shape
    row_count = depth * side_y * side_x
    slabs = lax.axis_size("slab")
    blocks, _ = refine_rows.shape
    capacity = max(2, (2 * blocks + slabs - 1) // slabs)

    up = [(i, i + 1) for i in range(slabs - 1)]
    down = [(i + 1, i) for i in range(slabs - 1)]
    before = lax.ppermute(tokens[-1:], "slab", up)
    after = lax.ppermute(tokens[:1], "slab", down)

    sent = pack(refine_dest[:, 0], refine_feat, refine_rows, slabs, capacity, row_count)
    received = lax.all_to_all(
        sent,
        "slab",
        split_axis=0,
        concat_axis=0,
        tiled=True,
    )

    base = conv(tokens, before, after, conv_w)
    weights = jnp.concatenate([w_val, w_gate], axis=1)

    mixed = scatter(base, received, capacity)
    assign, latent_new = mix(mixed, weights, latent_keys, norm_gain[None, :], latents)
    readback = jnp.dot(assign, latent_new.astype(BF16), preferred_element_type=F32)
    block_out = (mixed.astype(F32) + readback).astype(BF16)
    return (block_out.reshape(depth, side_y, side_x, width), latent_new)


def solution(mesh):
    return jax.shard_map(
        per_device,
        mesh=mesh,
        in_specs=(
            P("slab", None, None, "chan"),
            P("slab", None, "chan"),
            P("slab", None),
            P("slab", None),
            P(None, "chan"),
            P(),
            P(None, "chan"),
            P(None, "chan"),
            P(),
            P(None, "chan"),
        ),
        out_specs=(P("slab", None, None, "chan"), P(None, "chan")),
        check_vma=False,
    )
```
